32 devices in a mesh: grp: 2 (over y), ka: 4 (over z), vib: 2 (over core), fin: 2 (over x).
Axes of the slice: x: 2, y: 2, z: 4, core: 2. Of those that a mesh axis runs over, the one named last changes fastest.
Arguments:
- moments: bfloat16 [2, 2048, 2048], P(None, 'vib'), may hold values from -0.125 to 0.125
- initial_vectors: bfloat16 [8, 2048, 2048], P('ka', 'vib', 'grp'), parts along dimension 2, may hold values from -6 to 6
- final_vectors: bfloat16 [8, 2048, 1024], P('ka', 'vib', ('grp', 'fin')), parts along dimension 2, may hold values from -0.046875 to 0.046875
- basis_counts: int32 [16], P(('grp', 'ka')), parts along dimension 0, may hold values from 512 to 2048
Outputs:
- strengths: float32 [2048, 512], P(('grp', 'ka', 'vib'), 'fin'), parts along dimension 0
The draws below stay inside these ranges and needn't reach their ends.
There are 2 independent parts, one for each index of `grp`. The reference program is written for one: setup_inputs(seed, part) draws one part's arguments, and reference() takes and returns one part's arrays. A program takes and returns all parts, laid end to end along the dimension named above; an argument that names none is the same for every part. Nothing has to cross between parts.
All inputs are finite; a program needn't handle non-finite values.
Results may differ from the reference program's by a relative error of at most 0.0003.
Values may be sent and summed in bfloat16 or wider, within the bound.
A program may use at most 64 MiB of HBM per device.

```python
import jax
import jax.numpy as jnp
from jax import lax

NV = 2048
NI = 1024
NF = 512
JQ = 30
KB = 8


def place_ends(entries, rng, least, largest):
    extent = entries.shape
    spot = [jax.random.randint(jax.random.fold_in(rng, axis), (), 0, extent[axis]) for axis in range(len(extent))]
    entries = entries.at[tuple(spot)].set(least)
    longest = extent.index(max(extent))
    spot[longest] = (spot[longest] + 1) % extent[longest]
    return entries.at[tuple(spot)].set(largest)


def block_scale(stream_key, extent, shards, smallest, top_value):
    def one(axis_at, shards_of):
        steps = jax.random.uniform(jax.random.fold_in(jax.random.fold_in(stream_key, 6), axis_at), (shards_of,), jnp.float32, smallest / len(shards), top_value / len(shards))
        return jnp.repeat(jnp.exp(steps), extent[axis_at] // shards_of).reshape((-1,) + (1,) * (len(extent) - axis_at - 1))

    loudness = one(*shards[0])
    for cut in shards[1:]:
        loudness = loudness * one(*cut)
    return loudness


def gaussian(key, shape, deviation, limit, shards=(), held_as=jnp.bfloat16):
    drawn = jax.random.normal(key, shape, jnp.float32) * deviation
    if len(shards) > 0:
        drawn = block_scale(key, shape, shards, -0.22, 0.18) * drawn
    return jnp.clip(drawn, min=-limit, max=limit).astype(held_as)


def setup_inputs(seed: int = 0, part: int = 0) -> dict:
    streams_of = jax.random.split(jax.random.key(seed), 5)
    own_keys = jax.random.split(jax.random.fold_in(streams_of[4], part), 5)
    return {
        "moments": gaussian(streams_of[0], (2, NV, NV), NV ** -0.5, 0.125, ((1, 2),)),
        "initial_vectors": gaussian(own_keys[1], (KB, NV, NI), 1.0, 6.0, ((0, 4), (1, 2))),
        "final_vectors": gaussian(own_keys[2], (KB, NV, NF), (NV * KB) ** -0.5, 0.046875, ((0, 4), (1, 2), (2, 2))),
        "basis_counts": place_ends(jax.random.randint(own_keys[3], (KB,), NV // 4, NV + 1), jax.random.fold_in(own_keys[3], 1), NV // 4, NV).astype(jnp.int32),
    }


def reference(moments, initial_vectors, final_vectors, basis_counts):
    row_index = jnp.arange(NV, dtype=jnp.int32)
    keep_mask = row_index[None, :] < basis_counts[:, None]
    initial_live = jnp.where(keep_mask[:, :, None], initial_vectors, jnp.zeros((), initial_vectors.dtype))
    final_live = jnp.where(keep_mask[:, :, None], final_vectors, jnp.zeros((), final_vectors.dtype))
    moment_f32 = moments.astype(jnp.float32)

    def project_block(eigen_block):
        return jnp.einsum('cvw,vi->cwi', moment_f32, eigen_block.astype(jnp.float32), precision=lax.Precision.HIGHEST)
    projected = lax.map(project_block, initial_live)
    jsquare = float(JQ * (JQ + 1))
    norm_j = jnp.sqrt(jnp.float32(jsquare))
    k_value = (jnp.arange(KB, dtype=jnp.int32) - KB // 2).astype(jnp.float32)
    coef_same = k_value / norm_j
    coef_upper = 0.5 * jnp.sqrt(jsquare - k_value * (k_value + 1.0)) / norm_j
    coef_lower = -0.5 * jnp.sqrt(jsquare - k_value * (k_value - 1.0)) / norm_j
    along_z = projected[:, 0]
    along_x = projected[:, 1]
    zero_block = jnp.zeros_like(along_x[:1])
    upper_x = jnp.concatenate([along_x[1:], zero_block], axis=0)
    lower_x = jnp.concatenate([zero_block, along_x[:-1]], axis=0)
    coupled = coef_same[:, None, None] * along_z + coef_upper[:, None, None] * upper_x + coef_lower[:, None, None] * lower_x
    amplitude = jnp.einsum('kvf,kvi->if', final_live.astype(jnp.float32), coupled, precision=lax.Precision.HIGHEST)
    return amplitude * amplitude
```

```python
import functools

import jax
import jax.numpy as jnp
from jax import lax
from jax.experimental import pallas as pl
from jax.experimental.pallas import tpu as pltpu
from jax.sharding import PartitionSpec as P

JQ = 30
MESH = pl.DeviceIdType.MESH
F32 = jnp.float32
BF16 = jnp.bfloat16
LEVELS = 32767.0
TINY = 1e-30


def coefficient_rows(index, width):
    value = jnp.full((1, width), index, jnp.int32).astype(F32)
    jsquare = float(JQ * (JQ + 1))
    norm_j = jnp.sqrt(jnp.full((1, width), jsquare, F32))
    same = value / norm_j
    upper = 0.5 * jnp.sqrt(jsquare - value * (value + 1.0)) / norm_j
    lower = -0.5 * jnp.sqrt(jsquare - value * (value - 1.0)) / norm_j
    return same, upper, lower


def kernel(
    n_ka, n_half, chunks, counts_ref, moments_hbm, initial_hbm, final_hbm, out_ref,
    mom, ini, raw, own, edge, comb, split, amp, part, zsend, zrecv, ssend, srecv,
    mom_sem, ini_sem, raw_sem, own_send, own_recv, z_send, z_recv,
    fwd_send, fwd_recv, part_send, part_recv, out_send, out_recv, scale_send, scale_recv,
    token_up, token_down,
):
    kblocks, rows, width = raw.shape
    states = ini.shape[2]
    share = out_ref.shape[0]
    whole = mom.shape[2]
    half = width // n_half
    a = lax.axis_index("ka")
    b = lax.axis_index("vib")
    other = 1 - b
    first = a * kblocks - kblocks * n_ka // 2

    step = rows // chunks

    def get_final(h, j):
        span, lanes_h = pl.ds(j * step, step), pl.ds(h * half, half)
        return pltpu.make_async_copy(
            final_hbm.at[:, span, lanes_h], raw.at[:, span, lanes_h], raw_sem.at[h, j]
        )

    for h in range(n_half):
        for j in range(chunks):
            get_final(h, j).start()
    cores = (b, other)

    def cols_of(core):
        return pl.ds(pl.multiple_of(core * rows, rows), rows)

    def get_moments(i, c):
        span = cols_of(cores[i])
        return pltpu.make_async_copy(
            moments_hbm.at[c, :, span], mom.at[c, :, span], mom_sem.at[i, c]
        )

    for i in range(2):
        for c in range(2):
            get_moments(i, c).start()
    get_initial = pltpu.make_async_copy(initial_hbm, ini, ini_sem)
    get_initial.start()

    has_up = a < n_ka - 1
    has_down = a > 0
    sends = (has_up, has_down)
    takes = (has_down, has_up)
    toward_side = (a + 1, a - 1)

    barrier = pltpu.get_barrier_semaphore()
    pl.semaphore_signal(barrier, inc=1, device_id={"vib": other}, device_id_type=MESH)
    for side in range(2):
        @pl.when(sends[side])
        def _():
            pl.semaphore_signal(
                barrier, inc=1, device_id={"ka": toward_side[side]}, device_id_type=MESH
            )

    own_rows = cols_of(b)
    row_index = lax.broadcasted_iota(jnp.int32, (step, half), 0) + b * rows

    def mask_final(h, j):
        get_final(h, j).wait()
        for k in range(kblocks):
            live = row_index + j * step < counts_ref[k]
            piece = raw[k, j * step : (j + 1) * step, h * half : (h + 1) * half].astype(F32)
            own[h, at(b, j), k * half : (k + 1) * half] = jnp.where(live, piece, 0.0).astype(BF16)

    def at(core, j):
        return pl.ds(pl.multiple_of(core * rows + j * step, step), step)

    def side_lanes(side):
        return pl.ds(side * half, half)

    def z_copy(side, h, j):
        return pltpu.make_async_remote_copy(
            src_ref=own.at[h, at(b, j), side_lanes(1 - side)],
            dst_ref=edge.at[h, at(b, j), side_lanes(side)],
            send_sem=z_send.at[side, h, j],
            recv_sem=z_recv.at[side, h, j],
            device_id={"ka": toward_side[side]},
            device_id_type=MESH,
        )

    def forward(side, h, j):
        return pltpu.make_async_remote_copy(
            src_ref=edge.at[h, at(b, j), side_lanes(side)],
            dst_ref=edge.at[h, at(b, j), side_lanes(side)],
            send_sem=fwd_send.at[side, h, j],
            recv_sem=fwd_recv.at[side, h, j],
            device_id={"vib": other},
            device_id_type=MESH,
        )

    def own_copy(h):
        return pltpu.make_async_remote_copy(
            src_ref=own.at[h, own_rows],
            dst_ref=own.at[h, own_rows],
            send_sem=own_send.at[h],
            recv_sem=own_recv.at[h],
            device_id={"vib": other},
            device_id_type=MESH,
        )

    mask_final(0, 0)
    pl.semaphore_wait(barrier, 1 + has_up.astype(jnp.int32) + has_down.astype(jnp.int32))
    for h in range(n_half):
        for j in range(chunks):
            if h + j > 0:
                mask_final(h, j)
            for side in range(2):
                @pl.when(sends[side])
                def _():
                    z_copy(side, h, j).start()
        own_copy(h).start()
    for side in range(2):
        @pl.when(jnp.logical_not(takes[side]))
        def _():
            for h in range(n_half):
                edge[h, :, side * half : (side + 1) * half] = jnp.zeros((whole, half), BF16)

    same0, upper0, _ = coefficient_rows(first, half)
    same1, _, lower1 = coefficient_rows(first + 1, half)
    _, upper_below, _ = coefficient_rows(first - 1, half)
    _, _, lower_above = coefficient_rows(first + 2, half)
    same_row = jnp.concatenate([same0, same1], axis=1)
    cross_row = jnp.concatenate([lower1, upper0], axis=1)
    edge_row = jnp.concatenate([upper_below, lower_above], axis=1)

    def relay(h, j):
        for side in range(2):
            @pl.when(takes[side])
            def _():
                z_copy(side, h, j).wait_recv()
                forward(side, h, j).start()

    tile = rows // 2
    for i in range(2):
        for c in range(2):
            get_moments(i, c).wait()
        for h in range(n_half):
            if i == 1:
                own_copy(h).wait_recv()
            piece = own[h, cols_of(cores[i]), :]
            for t in range(2):
                span = pl.ds(t * tile, tile)
                along_z = jnp.dot(
                    mom[0, span, cols_of(cores[i])], piece, preferred_element_type=F32
                )
                along_x = jnp.dot(
                    mom[1, span, cols_of(cores[i])], piece, preferred_element_type=F32
                )
                crossed = jnp.concatenate([along_x[:, half:], along_x[:, :half]], axis=1)
                value = same_row * along_z + cross_row * crossed
                comb[h, span, :] = value if i == 0 else comb[h, span, :] + value

    def take(h, core, j):
        piece = edge[h, at(core, j), :]
        for t in range(2):
            span = pl.ds(t * tile, tile)
            comb[h, span, :] = comb[h, span, :] + edge_row * jnp.dot(
                mom[1, span, at(core, j)], piece, preferred_element_type=F32
            )

    block = min(256, rows)
    lane_index = lax.broadcasted_iota(jnp.int32, (half, block), 1) + b * rows

    def split_half(h):
        for t in range(rows // block):
            both = comb[h, pl.ds(t * block, block), :].T
            for k in range(kblocks):
                turned = both[k * half : (k + 1) * half]
                turned = jnp.where(lane_index + t * block < counts_ref[k], turned, 0.0)
                high = turned.astype(BF16)
                low = (turned - high.astype(F32)).astype(BF16)
                split[h, k, pl.ds(0, half), pl.ds(t * block, block)] = high
                split[h, k, pl.ds(half, half), pl.ds(t * block, block)] = low

    lanes = min(256, states)
    n_blocks = states // lanes
    targets = lanes // (2 * share)
    own_block = a // targets if targets > 1 else a

    toward = 2 * ((2 * a) // n_ka) - 1

    def block_of(s):
        return lax.rem(own_block + toward * (1 + s) + n_blocks, n_blocks)

    def part_copy(h, s):
        size = targets * share
        span = pl.ds(pl.multiple_of(block_of(s) * size, size), size)
        return pltpu.make_async_remote_copy(
            src_ref=amp.at[h, other, span],
            dst_ref=part.at[h, span],
            send_sem=part_send.at[h, s],
            recv_sem=part_recv.at[h, s],
            device_id={"vib": other},
            device_id_type=MESH,
        )

    def out_copies(h, sender, target, slot):
        values = pltpu.make_async_remote_copy(
            src_ref=zsend.at[h, slot],
            dst_ref=zrecv.at[h, sender],
            send_sem=out_send.at[h, slot],
            recv_sem=out_recv.at[h, sender],
            device_id={"ka": target},
            device_id_type=MESH,
        )
        scales = pltpu.make_async_remote_copy(
            src_ref=ssend.at[h, slot],
            dst_ref=srecv.at[h, sender],
            send_sem=scale_send.at[h, slot],
            recv_sem=scale_recv.at[h, sender],
            device_id={"ka": target},
            device_id_type=MESH,
        )
        return values, scales

    def token(side, r):
        to = toward_side[side]
        sem = (token_up, token_down)[side]
        about = a - 1 - r if side == 0 else a + 1 + r
        known = about >= 0 if side == 0 else about <= n_ka - 1

        @pl.when(jnp.logical_and(known, sends[side]))
        def _():
            pl.semaphore_signal(sem.at[r - 1], inc=1, device_id={"ka": to}, device_id_type=MESH)

    def await_token(side, r):
        sem = (token_up, token_down)[side]
        told = a - 2 - r >= 0 if side == 0 else a + 2 + r <= n_ka - 1

        @pl.when(told)
        def _():
            pl.semaphore_wait(sem.at[r - 1], 1)

    rounds = max(0, n_ka - 3)

    def finish(h, s):
        part_copy(h, s).wait_recv()
        for j in range(targets):
            target = block_of(s) * targets + j
            span = pl.ds(pl.multiple_of(target * share, share), share)
            slot = s * targets + j
            value = amp[h, b, span, :] + part[h, span, :]

            @pl.when(target == a)
            def _():
                out_ref[:, h * half : (h + 1) * half] = value

            @pl.when(target != a)
            def _():
                peak = jnp.maximum(jnp.max(jnp.abs(value), axis=0, keepdims=True), TINY)
                zsend[h, slot] = jnp.round(value * (LEVELS / peak)).astype(jnp.int16)
                ssend[h, slot] = jnp.broadcast_to(peak / LEVELS, (8, half))
                for copy in out_copies(h, a, target, slot):
                    copy.start()

    def amplitude_block(h, s):
        cols = pl.ds(pl.multiple_of(block_of(s) * lanes, lanes), lanes)
        both = jnp.dot(split[h, 0], ini[0, :, cols], preferred_element_type=F32)
        for k in range(1, kblocks):
            both = both + jnp.dot(split[h, k], ini[k, :, cols], preferred_element_type=F32)
        value = (both[:half] + both[half:]).T
        for j in range(targets):
            for core in range(2):
                low = (j * 2 + core) * share
                target = block_of(s) * targets + j
                amp[h, core, pl.ds(pl.multiple_of(target * share, share), share), :] = value[
                    low : low + share
                ]
        part_copy(h, s).start()

    for h in range(n_half):
        for j in range(chunks):
            if h == 0 or j > 0:
                relay(h, j)
            if h + j == 0 and rounds > 0:
                for side in range(2):
                    token(side, 1)
            take(h, b, j)
        for j in range(chunks):
            for side in range(2):
                @pl.when(takes[side])
                def _():
                    forward(side, h, j).wait_recv()
            take(h, other, j)
        split_half(h)
        if h == 0:
            get_initial.wait()
            for r in range(1, rounds + 1):
                for side in range(2):
                    if r > 1:
                        token(side, r)
                for side in range(2):
                    await_token(side, r)
        for s in range(n_blocks):
            amplitude_block(h, s)
            if s > 0:
                finish(h, s - 1)
            if s == n_blocks // 2 and h + 1 < n_half:
                relay(h + 1, 0)
    for h in range(n_half):
        finish(h, n_blocks - 1)

    for h in range(n_half):
        for d in range(1, n_ka):
            sender = lax.rem(a + d, n_ka)
            for copy in out_copies(h, sender, sender, 0):
                copy.wait_recv()
            lanes_h = pl.ds(h * half, half)
            out_ref[:, lanes_h] = out_ref[:, lanes_h] + (
                zrecv[h, sender].astype(F32) * srecv[h, sender, 0:1, :]
            )

    for h in range(n_half):
        own_copy(h).wait_send()
        for j in range(chunks):
            for side in range(2):
                @pl.when(sends[side])
                def _():
                    z_copy(side, h, j).wait_send()

                @pl.when(takes[side])
                def _():
                    forward(side, h, j).wait_send()
        for s in range(n_blocks):
            part_copy(h, s).wait_send()
            for j in range(targets):
                target = block_of(s) * targets + j

                @pl.when(target != a)
                def _():
                    for copy in out_copies(h, a, target, s * targets + j):
                        copy.wait_send()


def on_device(n_ka, moments, initial_vectors, final_vectors, basis_counts):
    kblocks, rows, states = initial_vectors.shape
    width = final_vectors.shape[2]
    whole = moments.shape[2]
    share = states // (2 * n_ka)
    n_half = max(1, width // 128)
    half = width // n_half
    chunks = 2
    dma = pltpu.SemaphoreType.DMA
    n_blocks = states // min(256, states)
    amplitude = pl.pallas_call(
        functools.partial(kernel, n_ka, n_half, chunks),
        out_shape=jax.ShapeDtypeStruct((share, width), F32),
        in_specs=[pl.BlockSpec(memory_space=pltpu.SMEM)]
        + [pl.BlockSpec(memory_space=pl.ANY)] * 3,
        out_specs=pl.BlockSpec(memory_space=pltpu.VMEM),
        scratch_shapes=[
            pltpu.VMEM(moments.shape, BF16),
            pltpu.VMEM(initial_vectors.shape, BF16),
            pltpu.VMEM(final_vectors.shape, BF16),
            pltpu.VMEM((n_half, whole, kblocks * half), BF16),
            pltpu.VMEM((n_half, whole, 2 * half), BF16),
            pltpu.VMEM((n_half, rows, kblocks * half), F32),
            pltpu.VMEM((n_half, kblocks, 2 * half, rows), BF16),
            pltpu.VMEM((n_half, 2, n_ka * share, half), F32),
            pltpu.VMEM((n_half, n_ka * share, half), F32),
            pltpu.VMEM((n_half, n_ka, share, half), jnp.int16),
            pltpu.VMEM((n_half, n_ka, share, half), jnp.int16),
            pltpu.VMEM((n_half, n_ka, 8, half), F32),
            pltpu.VMEM((n_half, n_ka, 8, half), F32),
            dma((2, 2)),
            dma(()),
            dma((n_half, chunks)),
            dma((n_half,)),
            dma((n_half,)),
            dma((2, n_half, chunks)),
            dma((2, n_half, chunks)),
            dma((2, n_half, chunks)),
            dma((2, n_half, chunks)),
            dma((n_half, n_blocks)),
            dma((n_half, n_blocks)),
            dma((n_half, n_ka)),
            dma((n_half, n_ka)),
            dma((n_half, n_ka)),
            dma((n_half, n_ka)),
            pltpu.SemaphoreType.REGULAR((max(1, n_ka - 3),)),
            pltpu.SemaphoreType.REGULAR((max(1, n_ka - 3),)),
        ],
        compiler_params=pltpu.CompilerParams(
            collective_id=0, has_side_effects=True, vmem_limit_bytes=60 * 2**20
        ),
    )(basis_counts, moments, initial_vectors, final_vectors)
    return amplitude * amplitude


def solution(mesh):
    in_specs = (
        P(None, "vib", None),
        P("ka", "vib", "grp"),
        P("ka", "vib", ("grp", "fin")),
        P(("grp", "ka")),
    )
    out_specs = P(("grp", "ka", "vib"), "fin")
    return jax.shard_map(
        functools.partial(on_device, mesh.shape["ka"]),
        mesh=mesh, in_specs=in_specs, out_specs=out_specs, check_vma=False,
    )
```

```python
import functools

import jax
import jax.numpy as jnp
from jax import lax
from jax.experimental import pallas as pl
from jax.experimental.pallas import tpu as pltpu
from jax.sharding import PartitionSpec as P

JQ = 30
MESH = pl.DeviceIdType.MESH
F32 = jnp.float32
BF16 = jnp.bfloat16
LEVELS = 32767.0
TINY = 1e-30


def coefficient_rows(index, width):
    value = jnp.full((1, width), index, jnp.int32).astype(F32)
    jsquare = float(JQ * (JQ + 1))
    norm_j = jnp.sqrt(jnp.full((1, width), jsquare, F32))
    same = value / norm_j
    upper = 0.5 * jnp.sqrt(jsquare - value * (value + 1.0)) / norm_j
    lower = -0.5 * jnp.sqrt(jsquare - value * (value - 1.0)) / norm_j
    return same, upper, lower


def kernel(
    n_ka, n_half, chunks, parts, counts_ref, moments_hbm, initial_hbm, final_hbm, out_ref,
    mom, ini, turned, own, edge, comb, split, amp, part, zsend, zrecv, ssend, srecv, csend, crecv,
    mom_sem, ini_sem, own_sem, own_send, own_recv, z_send, z_recv, count_send, count_recv,
    fwd_send, fwd_recv, part_send, part_recv, out_send, out_recv, scale_send, scale_recv,
    token_up, token_down,
):
    kblocks, rows, states = ini.shape
    width = final_hbm.shape[2]
    share = out_ref.shape[0]
    whole = mom.shape[2]
    half = width // n_half
    a = lax.axis_index("ka")
    b = lax.axis_index("vib")
    other = 1 - b
    first = a * kblocks - kblocks * n_ka // 2

    step = rows // chunks
    last = kblocks - 1
    cores = (b, other)

    def cols_of(core):
        return pl.ds(pl.multiple_of(core * rows, rows), rows)

    def get_moments(i, c):
        span = cols_of(cores[i])
        return pltpu.make_async_copy(
            moments_hbm.at[c, :, span], mom.at[c, :, span], mom_sem.at[i, c]
        )

    def half_lanes(k):
        return pl.ds(k * half, half)

    def get_own(h, k):
        return pltpu.make_async_copy(
            final_hbm.at[k, :, half_lanes(h)], own.at[h, cols_of(b), half_lanes(k)], own_sem.at[h, k]
        )

    for h in range(n_half):
        for k in range(kblocks):
            get_own(h, k).start()
    for i in range(2):
        for c in range(2):
            get_moments(i, c).start()
    get_initial = pltpu.make_async_copy(initial_hbm, ini, ini_sem)
    get_initial.start()

    has_up = a < n_ka - 1
    has_down = a > 0
    sends = (has_up, has_down)
    takes = (has_down, has_up)
    toward_side = (a + 1, a - 1)

    barrier = pltpu.get_barrier_semaphore()
    pl.semaphore_signal(barrier, inc=1, device_id={"vib": other}, device_id_type=MESH)
    for side in range(2):
        @pl.when(sends[side])
        def _():
            pl.semaphore_signal(
                barrier, inc=1, device_id={"ka": toward_side[side]}, device_id_type=MESH
            )

    def at(core, j):
        return pl.ds(pl.multiple_of(core * rows + j * step, step), step)

    def z_copy(side, h, j):
        return pltpu.make_async_remote_copy(
            src_ref=final_hbm.at[last * (1 - side), pl.ds(j * step, step), half_lanes(h)],
            dst_ref=edge.at[h, at(b, j), half_lanes(side)],
            send_sem=z_send.at[side, h, j],
            recv_sem=z_recv.at[side, h, j],
            device_id={"ka": toward_side[side]},
            device_id_type=MESH,
        )

    def count_copy(side):
        return pltpu.make_async_remote_copy(
            src_ref=csend.at[side],
            dst_ref=crecv.at[side],
            send_sem=count_send.at[side],
            recv_sem=count_recv.at[side],
            device_id={"ka": toward_side[side]},
            device_id_type=MESH,
        )

    def forward(side, h, j):
        return pltpu.make_async_remote_copy(
            src_ref=edge.at[h, at(b, j), half_lanes(side)],
            dst_ref=edge.at[h, at(b, j), half_lanes(side)],
            send_sem=fwd_send.at[side, h, j],
            recv_sem=fwd_recv.at[side, h, j],
            device_id={"vib": other},
            device_id_type=MESH,
        )

    def own_copy(h, k):
        return pltpu.make_async_remote_copy(
            src_ref=final_hbm.at[k, :, half_lanes(h)],
            dst_ref=own.at[h, cols_of(b), half_lanes(k)],
            send_sem=own_send.at[h, k],
            recv_sem=own_recv.at[h, k],
            device_id={"vib": other},
            device_id_type=MESH,
        )

    for side in range(2):
        csend[side] = jnp.full(csend.shape[1:], counts_ref[last * (1 - side)], jnp.int32)

        @pl.when(jnp.logical_not(takes[side]))
        def _():
            crecv[side] = jnp.zeros(crecv.shape[1:], jnp.int32)
            for h in range(n_half):
                edge[h, :, side * half : (side + 1) * half] = jnp.zeros((whole, half), BF16)

    pl.semaphore_wait(barrier, 1 + has_up.astype(jnp.int32) + has_down.astype(jnp.int32))
    for side in range(2):
        @pl.when(sends[side])
        def _():
            count_copy(side).start()
    for h in range(n_half):
        for j in range(chunks):
            for side in range(2):
                @pl.when(sends[side])
                def _():
                    z_copy(side, h, j).start()
    for h in range(n_half):
        for k in range(kblocks):
            own_copy(h, k).start()

    same0, upper0, _ = coefficient_rows(first, half)
    same1, _, lower1 = coefficient_rows(first + 1, half)
    _, upper_below, _ = coefficient_rows(first - 1, half)
    _, _, lower_above = coefficient_rows(first + 2, half)
    same_row = jnp.concatenate([same0, same1], axis=1)
    cross_row = jnp.concatenate([lower1, upper0], axis=1)
    edge_row = jnp.concatenate([upper_below, lower_above], axis=1)

    def relay(h, j):
        for side in range(2):
            @pl.when(takes[side])
            def _():
                z_copy(side, h, j).wait_recv()
                forward(side, h, j).start()

    tile = rows // 2
    for i in range(2):
        row_index = lax.broadcasted_iota(jnp.int32, (rows, half), 0) + cores[i] * rows
        for h in range(n_half):
            masked = []
            for k in range(kblocks):
                if i == 0:
                    get_own(h, k).wait()
                else:
                    own_copy(h, k).wait_recv()
                piece = own[h, cols_of(cores[i]), half_lanes(k)].astype(F32)
                masked.append(jnp.where(row_index < counts_ref[k], piece, 0.0).astype(BF16))
            piece = jnp.concatenate(masked, axis=1)
            if h == 0:
                for c in range(2):
                    get_moments(i, c).wait()
            for t in range(2):
                span = pl.ds(t * tile, tile)
                along_z = jnp.dot(
                    mom[0, span, cols_of(cores[i])], piece, preferred_element_type=F32
                )
                along_x = jnp.dot(
                    mom[1, span, cols_of(cores[i])], piece, preferred_element_type=F32
                )
                crossed = jnp.concatenate([along_x[:, half:], along_x[:, :half]], axis=1)
                value = same_row * along_z + cross_row * crossed
                comb[h, span, :] = value if i == 0 else comb[h, span, :] + value

    get_initial.wait()
    block = min(256, rows)
    for k in range(kblocks):
        for v in range(rows // block):
            low = k * rows + v * block
            turned[:, low : low + block] = ini[k, v * block : (v + 1) * block, :].T

    for side in range(2):
        @pl.when(takes[side])
        def _():
            count_copy(side).wait_recv()
    edge_counts = jnp.concatenate([crecv[0, 0:1, :], crecv[1, 0:1, :]], axis=1)
    edge_index = lax.broadcasted_iota(jnp.int32, (step, 2 * half), 0)

    def take(h, core, j):
        live = edge_index + (core * rows + j * step) < edge_counts
        piece = jnp.where(live, edge[h, at(core, j), :].astype(F32), 0.0).astype(BF16)
        for t in range(2):
            span = pl.ds(t * tile, tile)
            comb[h, span, :] = comb[h, span, :] + edge_row * jnp.dot(
                mom[1, span, at(core, j)], piece, preferred_element_type=F32
            )

    row_index = lax.broadcasted_iota(jnp.int32, (block, half), 0) + b * rows

    def split_half(h):
        for v in range(rows // block):
            for k in range(kblocks):
                value = comb[h, v * block : (v + 1) * block, k * half : (k + 1) * half]
                value = jnp.where(row_index + v * block < counts_ref[k], value, 0.0)
                high = value.astype(BF16)
                low = (value - high.astype(F32)).astype(BF16)
                start = k * rows + v * block
                split[h, start : start + block, 0:half] = high
                split[h, start : start + block, half:] = low

    targets = n_ka // parts
    size = targets * share

    toward = (2 * a) // n_ka

    def part_of(s):
        return lax.rem(toward + 1 + s, parts)

    def part_copy(h, s):
        span = pl.ds(pl.multiple_of(part_of(s) * size, size), size)
        return pltpu.make_async_remote_copy(
            src_ref=amp.at[h, other, span],
            dst_ref=part.at[h, span],
            send_sem=part_send.at[h, s],
            recv_sem=part_recv.at[h, s],
            device_id={"vib": other},
            device_id_type=MESH,
        )

    def target_of(s, j):
        return part_of(s) * targets + (1 - toward) * (targets - 1 - j) + toward * j

    def out_copies(h, sender, target, slot):
        values = pltpu.make_async_remote_copy(
            src_ref=zsend.at[h, slot],
            dst_ref=zrecv.at[h, sender],
            send_sem=out_send.at[h, slot],
            recv_sem=out_recv.at[h, sender],
            device_id={"ka": target},
            device_id_type=MESH,
        )
        scales = pltpu.make_async_remote_copy(
            src_ref=ssend.at[h, slot],
            dst_ref=srecv.at[h, sender],
            send_sem=scale_send.at[h, slot],
            recv_sem=scale_recv.at[h, sender],
            device_id={"ka": target},
            device_id_type=MESH,
        )
        return values, scales

    def token(side, r):
        to = toward_side[side]
        sem = (token_up, token_down)[side]
        about = a - 1 - r if side == 0 else a + 1 + r
        known = about >= 0 if side == 0 else about <= n_ka - 1

        @pl.when(jnp.logical_and(known, sends[side]))
        def _():
            pl.semaphore_signal(sem.at[r - 1], inc=1, device_id={"ka": to}, device_id_type=MESH)

    def await_token(side, r):
        sem = (token_up, token_down)[side]
        told = a - 2 - r >= 0 if side == 0 else a + 2 + r <= n_ka - 1

        @pl.when(told)
        def _():
            pl.semaphore_wait(sem.at[r - 1], 1)

    rounds = max(0, n_ka - 3)

    def finish(h, s):
        part_copy(h, s).wait_recv()
        for j in range(targets):
            target = target_of(s, j)
            span = pl.ds(pl.multiple_of(target * share, share), share)
            slot = s * targets + j
            value = amp[h, b, span, :] + part[h, span, :]

            @pl.when(target == a)
            def _():
                out_ref[:, h * half : (h + 1) * half] = value

            @pl.when(target != a)
            def _():
                peak = jnp.maximum(jnp.max(jnp.abs(value), axis=0, keepdims=True), TINY)
                zsend[h, slot] = jnp.round(value * (LEVELS / peak)).astype(jnp.int16)
                ssend[h, slot] = jnp.broadcast_to(peak / LEVELS, (8, half))
                for copy in out_copies(h, a, target, slot):
                    copy.start()

    def amplitude_block(h, s):
        lanes = states // parts
        span = pl.ds(pl.multiple_of(part_of(s) * lanes, lanes), lanes)
        both = jnp.dot(turned[span, :], split[h], preferred_element_type=F32)
        value = both[:, :half] + both[:, half:]
        for j in range(targets):
            for core in range(2):
                low = (j * 2 + core) * share
                target = part_of(s) * targets + j
                amp[h, core, pl.ds(pl.multiple_of(target * share, share), share), :] = value[
                    low : low + share
                ]
        part_copy(h, s).start()

    for h in range(n_half):
        for j in range(chunks):
            if h == 0 or j > 0:
                relay(h, j)
            if h + j == 0 and rounds > 0:
                for side in range(2):
                    token(side, 1)
            take(h, b, j)
        for j in range(chunks):
            for side in range(2):
                @pl.when(takes[side])
                def _():
                    forward(side, h, j).wait_recv()
            take(h, other, j)
        split_half(h)
        if h == 0:
            for r in range(1, rounds + 1):
                for side in range(2):
                    if r > 1:
                        token(side, r)
                for side in range(2):
                    await_token(side, r)
        for s in range(parts):
            amplitude_block(h, s)
            if s > 0:
                finish(h, s - 1)
            if s == 0 and h + 1 < n_half:
                relay(h + 1, 0)
    for h in range(n_half):
        finish(h, parts - 1)

    for h in range(n_half):
        for d in range(1, n_ka):
            sender = lax.rem(a + d, n_ka)
            for copy in out_copies(h, sender, sender, 0):
                copy.wait_recv()
            lanes_h = pl.ds(h * half, half)
            out_ref[:, lanes_h] = out_ref[:, lanes_h] + (
                zrecv[h, sender].astype(F32) * srecv[h, sender, 0:1, :]
            )

    for side in range(2):
        @pl.when(sends[side])
        def _():
            count_copy(side).wait_send()

    for h in range(n_half):
        for k in range(kblocks):
            own_copy(h, k).wait_send()
        for j in range(chunks):
            for side in range(2):
                @pl.when(sends[side])
                def _():
                    z_copy(side, h, j).wait_send()

                @pl.when(takes[side])
                def _():
                    forward(side, h, j).wait_send()
        for s in range(parts):
            part_copy(h, s).wait_send()
            for j in range(targets):
                target = target_of(s, j)

                @pl.when(target != a)
                def _():
                    for copy in out_copies(h, a, target, s * targets + j):
                        copy.wait_send()


def on_device(n_ka, moments, initial_vectors, final_vectors, basis_counts):
    kblocks, rows, states = initial_vectors.shape
    width = final_vectors.shape[2]
    whole = moments.shape[2]
    share = states // (2 * n_ka)
    n_half = max(1, width // 128)
    half = width // n_half
    chunks = 2
    dma = pltpu.SemaphoreType.DMA
    parts = 2
    amplitude = pl.pallas_call(
        functools.partial(kernel, n_ka, n_half, chunks, parts),
        out_shape=jax.ShapeDtypeStruct((share, width), F32),
        in_specs=[pl.BlockSpec(memory_space=pltpu.SMEM)]
        + [pl.BlockSpec(memory_space=pl.ANY)] * 3,
        out_specs=pl.BlockSpec(memory_space=pltpu.VMEM),
        scratch_shapes=[
            pltpu.VMEM(moments.shape, BF16),
            pltpu.VMEM(initial_vectors.shape, BF16),
            pltpu.VMEM((states, kblocks * rows), BF16),
            pltpu.VMEM((n_half, whole, kblocks * half), BF16),
            pltpu.VMEM((n_half, whole, 2 * half), BF16),
            pltpu.VMEM((n_half, rows, kblocks * half), F32),
            pltpu.VMEM((n_half, kblocks * rows, 2 * half), BF16),
            pltpu.VMEM((n_half, 2, n_ka * share, half), F32),
            pltpu.VMEM((n_half, n_ka * share, half), F32),
            pltpu.VMEM((n_half, n_ka, share, half), jnp.int16),
            pltpu.VMEM((n_half, n_ka, share, half), jnp.int16),
            pltpu.VMEM((n_half, n_ka, 8, half), F32),
            pltpu.VMEM((n_half, n_ka, 8, half), F32),
            pltpu.VMEM((2, 8, half), jnp.int32),
            pltpu.VMEM((2, 8, half), jnp.int32),
            dma((2, 2)),
            dma(()),
            dma((n_half, kblocks)),
            dma((n_half, kblocks)),
            dma((n_half, kblocks)),
            dma((2, n_half, chunks)),
            dma((2, n_half, chunks)),
            dma((2,)),
            dma((2,)),
            dma((2, n_half, chunks)),
            dma((2, n_half, chunks)),
            dma((n_half, parts)),
            dma((n_half, parts)),
            dma((n_half, n_ka)),
            dma((n_half, n_ka)),
            dma((n_half, n_ka)),
            dma((n_half, n_ka)),
            pltpu.SemaphoreType.REGULAR((max(1, n_ka - 3),)),
            pltpu.SemaphoreType.REGULAR((max(1, n_ka - 3),)),
        ],
        compiler_params=pltpu.CompilerParams(
            collective_id=0, has_side_effects=True, vmem_limit_bytes=60 * 2**20
        ),
    )(basis_counts, moments, initial_vectors, final_vectors)
    return amplitude * amplitude


def solution(mesh):
    in_specs = (
        P(None, "vib", None),
        P("ka", "vib", "grp"),
        P("ka", "vib", ("grp", "fin")),
        P(("grp", "ka")),
    )
    out_specs = P(("grp", "ka", "vib"), "fin")
    return jax.shard_map(
        functools.partial(on_device, mesh.shape["ka"]),
        mesh=mesh, in_specs=in_specs, out_specs=out_specs, check_vma=False,
    )
```

```python
import functools

import jax
import jax.numpy as jnp
from jax import lax
from jax.experimental import pallas as pl
from jax.experimental.pallas import tpu as pltpu
from jax.sharding import PartitionSpec as P

JQ = 30
MESH = pl.DeviceIdType.MESH
F32 = jnp.float32
BF16 = jnp.bfloat16
LEVELS = 32767.0
TINY = 1e-30


def coefficient_rows(index, width):
    value = jnp.full((1, width), index, jnp.int32).astype(F32)
    jsquare = float(JQ * (JQ + 1))
    norm_j = jnp.sqrt(jnp.full((1, width), jsquare, F32))
    same = value / norm_j
    upper = 0.5 * jnp.sqrt(jsquare - value * (value + 1.0)) / norm_j
    lower = -0.5 * jnp.sqrt(jsquare - value * (value - 1.0)) / norm_j
    return same, upper, lower


def kernel(
    n_ka, n_half, chunks, parts, counts_ref, moments_hbm, initial_hbm, final_hbm, out_ref,
    mom, ini, turned, own, edge, comb, split, amp, part, zsend, zrecv, ssend, srecv, csend, crecv,
    mom_sem, ini_sem, own_sem, own_send, own_recv, z_send, z_recv, count_send, count_recv,
    fwd_send, fwd_recv, part_send, part_recv, out_send, out_recv, scale_send, scale_recv,
    token_up, token_down,
):
    kblocks, rows, states = ini.shape
    width = final_hbm.shape[2]
    share = out_ref.shape[0]
    whole = mom.shape[2]
    half = width // n_half
    a = lax.axis_index("ka")
    b = lax.axis_index("vib")
    other = 1 - b
    first = a * kblocks - kblocks * n_ka // 2

    has_up = a < n_ka - 1
    has_down = a > 0
    sends = (has_up, has_down)
    takes = (has_down, has_up)
    toward_side = (a + 1, a - 1)

    barrier = pltpu.get_barrier_semaphore()
    pl.semaphore_signal(barrier, inc=1, device_id={"vib": other}, device_id_type=MESH)
    for side in range(2):
        @pl.when(sends[side])
        def _():
            pl.semaphore_signal(
                barrier, inc=1, device_id={"ka": toward_side[side]}, device_id_type=MESH
            )

    step = rows // chunks
    last = kblocks - 1
    cores = (b, other)

    def cols_of(core):
        return pl.ds(pl.multiple_of(core * rows, rows), rows)

    def get_moments(i, c):
        span = cols_of(cores[i])
        return pltpu.make_async_copy(
            moments_hbm.at[c, :, span], mom.at[c, :, span], mom_sem.at[i, c]
        )

    def half_lanes(k):
        return pl.ds(k * half, half)

    def get_own(h, k):
        return pltpu.make_async_copy(
            final_hbm.at[k, :, half_lanes(h)], own.at[h, cols_of(b), half_lanes(k)], own_sem.at[h, k]
        )

    for h in range(n_half):
        for k in range(kblocks):
            get_own(h, k).start()
    for i in range(2):
        for c in range(2):
            get_moments(i, c).start()
    get_initial = pltpu.make_async_copy(initial_hbm, ini, ini_sem)

    def at(core, j):
        return pl.ds(pl.multiple_of(core * rows + j * step, step), step)

    def z_copy(side, h, j):
        return pltpu.make_async_remote_copy(
            src_ref=final_hbm.at[last * (1 - side), pl.ds(j * step, step), half_lanes(h)],
            dst_ref=edge.at[h, at(b, j), half_lanes(side)],
            send_sem=z_send.at[side, h, j],
            recv_sem=z_recv.at[side, h, j],
            device_id={"ka": toward_side[side]},
            device_id_type=MESH,
        )

    def count_copy(side):
        return pltpu.make_async_remote_copy(
            src_ref=csend.at[side],
            dst_ref=crecv.at[side],
            send_sem=count_send.at[side],
            recv_sem=count_recv.at[side],
            device_id={"ka": toward_side[side]},
            device_id_type=MESH,
        )

    def forward(side, h, j):
        return pltpu.make_async_remote_copy(
            src_ref=edge.at[h, at(b, j), half_lanes(side)],
            dst_ref=edge.at[h, at(b, j), half_lanes(side)],
            send_sem=fwd_send.at[side, h, j],
            recv_sem=fwd_recv.at[side, h, j],
            device_id={"vib": other},
            device_id_type=MESH,
        )

    def own_copy(h, k):
        return pltpu.make_async_remote_copy(
            src_ref=final_hbm.at[k, :, half_lanes(h)],
            dst_ref=own.at[h, cols_of(b), half_lanes(k)],
            send_sem=own_send.at[h, k],
            recv_sem=own_recv.at[h, k],
            device_id={"vib": other},
            device_id_type=MESH,
        )

    for side in range(2):
        csend[side] = jnp.full(csend.shape[1:], counts_ref[last * (1 - side)], jnp.int32)

        @pl.when(jnp.logical_not(takes[side]))
        def _():
            crecv[side] = jnp.zeros(crecv.shape[1:], jnp.int32)
            for h in range(n_half):
                edge[h, :, side * half : (side + 1) * half] = jnp.zeros((whole, half), BF16)

    pl.semaphore_wait(barrier, 1 + has_up.astype(jnp.int32) + has_down.astype(jnp.int32))
    for side in range(2):
        @pl.when(sends[side])
        def _():
            count_copy(side).start()
    for h in range(n_half):
        for j in range(chunks):
            for side in range(2):
                @pl.when(sends[side])
                def _():
                    z_copy(side, h, j).start()
    for h in range(n_half):
        for k in range(kblocks):
            own_copy(h, k).start()

    same0, upper0, _ = coefficient_rows(first, half)
    same1, _, lower1 = coefficient_rows(first + 1, half)
    _, upper_below, _ = coefficient_rows(first - 1, half)
    _, _, lower_above = coefficient_rows(first + 2, half)
    same_row = jnp.concatenate([same0, same1], axis=1)
    cross_row = jnp.concatenate([lower1, upper0], axis=1)
    edge_row = jnp.concatenate([upper_below, lower_above], axis=1)

    def token(side, r):
        to = toward_side[side]
        sem = (token_up, token_down)[side]
        about = a - 1 - r if side == 0 else a + 1 + r
        known = about >= 0 if side == 0 else about <= n_ka - 1

        @pl.when(jnp.logical_and(known, sends[side]))
        def _():
            pl.semaphore_signal(sem.at[r - 1], inc=1, device_id={"ka": to}, device_id_type=MESH)

    def await_token(side, r):
        sem = (token_up, token_down)[side]
        told = a - 2 - r >= 0 if side == 0 else a + 2 + r <= n_ka - 1

        @pl.when(told)
        def _():
            pl.semaphore_wait(sem.at[r - 1], 1)

    rounds = max(0, n_ka - 3)

    def relay(h, j):
        for side in range(2):
            @pl.when(takes[side])
            def _():
                z_copy(side, h, j).wait_recv()
                forward(side, h, j).start()

    tile = min(256, rows)

    def own_piece(i, h):
        row_index = lax.broadcasted_iota(jnp.int32, (rows, half), 0) + cores[i] * rows
        masked = []
        for k in range(kblocks):
            if i == 0:
                get_own(h, k).wait()
            else:
                own_copy(h, k).wait_recv()
            piece = own[h, cols_of(cores[i]), half_lanes(k)].astype(F32)
            masked.append(jnp.where(row_index < counts_ref[k], piece, 0.0).astype(BF16))
        return jnp.concatenate(masked, axis=1)

    def moments_ready(i):
        for c in range(2):
            get_moments(i, c).wait()

    def own_half(i, h):
        piece = own_piece(i, h)
        if h == 0:
            moments_ready(i)
            if i == 0:
                get_initial.start()
        for t in range(rows // tile):
            span = pl.ds(t * tile, tile)
            along_z = jnp.dot(mom[0, span, cols_of(cores[i])], piece, preferred_element_type=F32)
            along_x = jnp.dot(mom[1, span, cols_of(cores[i])], piece, preferred_element_type=F32)
            crossed = jnp.concatenate([along_x[:, half:], along_x[:, :half]], axis=1)
            value = same_row * along_z + cross_row * crossed
            comb[h, span, :] = value if i == 0 else comb[h, span, :] + value

    for i in range(2):
        for h in range(n_half):
            own_half(i, h)

    early = (chunks + 1) // 2
    for j in range(early):
        relay(0, j)
    if rounds > 0:
        for side in range(2):
            token(side, 1)

    block = min(256, rows)

    def turn_initial():
        get_initial.wait()
        for k in range(kblocks):
            for v in range(rows // block):
                low = k * rows + v * block
                turned[:, low : low + block] = ini[k, v * block : (v + 1) * block, :].T

    turn_initial()

    for side in range(2):
        @pl.when(takes[side])
        def _():
            count_copy(side).wait_recv()
    edge_counts = jnp.concatenate([crecv[0, 0:1, :], crecv[1, 0:1, :]], axis=1)
    edge_index = lax.broadcasted_iota(jnp.int32, (step, 2 * half), 0)

    def take(h, core, j):
        live = edge_index + (core * rows + j * step) < edge_counts
        piece = jnp.where(live, edge[h, at(core, j), :].astype(F32), 0.0).astype(BF16)
        for t in range(rows // tile):
            span = pl.ds(t * tile, tile)
            comb[h, span, :] = comb[h, span, :] + edge_row * jnp.dot(
                mom[1, span, at(core, j)], piece, preferred_element_type=F32
            )

    row_index = lax.broadcasted_iota(jnp.int32, (block, half), 0) + b * rows

    def split_half(h):
        for v in range(rows // block):
            for k in range(kblocks):
                value = comb[h, v * block : (v + 1) * block, k * half : (k + 1) * half]
                value = jnp.where(row_index + v * block < counts_ref[k], value, 0.0)
                high = value.astype(BF16)
                low = (value - high.astype(F32)).astype(BF16)
                start = k * rows + v * block
                split[h, start : start + block, 0:half] = high
                split[h, start : start + block, half:] = low

    targets = n_ka // parts
    size = targets * share

    def part_copy(h, s):
        span = pl.ds(s * size, size)
        return pltpu.make_async_remote_copy(
            src_ref=amp.at[h, other, span],
            dst_ref=part.at[h, span],
            send_sem=part_send.at[h, s],
            recv_sem=part_recv.at[h, s],
            device_id={"vib": other},
            device_id_type=MESH,
        )

    def out_copies(h, sender, target, slot):
        values = pltpu.make_async_remote_copy(
            src_ref=zsend.at[h, slot],
            dst_ref=zrecv.at[h, sender],
            send_sem=out_send.at[h, slot],
            recv_sem=out_recv.at[h, sender],
            device_id={"ka": target},
            device_id_type=MESH,
        )
        scales = pltpu.make_async_remote_copy(
            src_ref=ssend.at[h, slot],
            dst_ref=srecv.at[h, sender],
            send_sem=scale_send.at[h, slot],
            recv_sem=scale_recv.at[h, sender],
            device_id={"ka": target},
            device_id_type=MESH,
        )
        return values, scales

    def finish(h, s):
        part_copy(h, s).wait_recv()
        for j in range(targets):
            target = s * targets + j
            span = pl.ds(target * share, share)
            value = amp[h, b, span, :] + part[h, span, :]

            @pl.when(target == a)
            def _():
                out_ref[:, h * half : (h + 1) * half] = value

            @pl.when(target != a)
            def _():
                peak = jnp.maximum(jnp.max(jnp.abs(value), axis=0, keepdims=True), TINY)
                zsend[h, target] = jnp.round(value * (LEVELS / peak)).astype(jnp.int16)
                ssend[h, target] = jnp.broadcast_to(peak / LEVELS, (8, half))
                for copy in out_copies(h, a, target, target):
                    copy.start()

    def amplitude_block(h, s):
        lanes = states // parts
        for q in range(lanes // tile):
            low = s * lanes + q * tile
            both = jnp.dot(turned[low : low + tile, :], split[h], preferred_element_type=F32)
            value = both[:, :half] + both[:, half:]
            for piece in range(tile // share):
                target, core = divmod(low // share + piece, 2)
                amp[h, core, pl.ds(target * share, share), :] = value[
                    piece * share : (piece + 1) * share
                ]
        part_copy(h, s).start()

    def take_other(h, j):
        for side in range(2):
            @pl.when(takes[side])
            def _():
                forward(side, h, j).wait_recv()
        take(h, other, j)

    for h in range(n_half):
        for j in range(chunks):
            if h > 0 or j >= early:
                relay(h, j)
            take(h, b, j)
            if h > 0 and j == 0:
                finish(h - 1, parts - 1)
            if j > 0:
                take_other(h, j - 1)
        take_other(h, chunks - 1)
        split_half(h)
        if h == 0:
            for r in range(1, rounds + 1):
                for side in range(2):
                    if r > 1:
                        token(side, r)
                for side in range(2):
                    await_token(side, r)
        for s in range(parts):
            amplitude_block(h, s)
        for s in range(parts - 1):
            finish(h, s)
    finish(n_half - 1, parts - 1)

    def add_sums(h, d):
        sender = lax.rem(a + d, n_ka)
        for copy in out_copies(h, sender, sender, 0):
            copy.wait_recv()
        lanes_h = half_lanes(h)
        out_ref[:, lanes_h] = out_ref[:, lanes_h] + (
            zrecv[h, sender].astype(F32) * srecv[h, sender, 0:1, :]
        )

    for h in range(n_half):
        for d in range(1, n_ka):
            add_sums(h, d)

    def drain():
        for side in range(2):
            @pl.when(sends[side])
            def _():
                count_copy(side).wait_send()

        for h in range(n_half):
            for k in range(kblocks):
                own_copy(h, k).wait_send()
            for j in range(chunks):
                for side in range(2):
                    @pl.when(sends[side])
                    def _():
                        z_copy(side, h, j).wait_send()

                    @pl.when(takes[side])
                    def _():
                        forward(side, h, j).wait_send()
            for s in range(parts):
                part_copy(h, s).wait_send()
                for j in range(targets):
                    target = s * targets + j

                    @pl.when(target != a)
                    def _():
                        for copy in out_copies(h, a, target, target):
                            copy.wait_send()


    drain()


def on_device(n_ka, moments, initial_vectors, final_vectors, basis_counts):
    kblocks, rows, states = initial_vectors.shape
    width = final_vectors.shape[2]
    whole = moments.shape[2]
    share = states // (2 * n_ka)
    n_half = max(1, width // 128)
    half = width // n_half
    chunks = 2
    dma = pltpu.SemaphoreType.DMA
    parts = 2
    amplitude = pl.pallas_call(
        functools.partial(kernel, n_ka, n_half, chunks, parts),
        out_shape=pltpu.VMEM((share, width), F32),
        in_specs=[pl.BlockSpec(memory_space=pltpu.SMEM)]
        + [pl.BlockSpec(memory_space=pl.ANY)] * 3,
        out_specs=pl.BlockSpec(memory_space=pltpu.VMEM),
        scratch_shapes=[
            pltpu.VMEM(moments.shape, BF16),
            pltpu.VMEM(initial_vectors.shape, BF16),
            pltpu.VMEM((states, kblocks * rows), BF16),
            pltpu.VMEM((n_half, whole, kblocks * half), BF16),
            pltpu.VMEM((n_half, whole, 2 * half), BF16),
            pltpu.VMEM((n_half, rows, kblocks * half), F32),
            pltpu.VMEM((n_half, kblocks * rows, 2 * half), BF16),
            pltpu.VMEM((n_half, 2, n_ka * share, half), F32),
            pltpu.VMEM((n_half, n_ka * share, half), F32),
            pltpu.VMEM((n_half, n_ka, share, half), jnp.int16),
            pltpu.VMEM((n_half, n_ka, share, half), jnp.int16),
            pltpu.VMEM((n_half, n_ka, 8, half), F32),
            pltpu.VMEM((n_half, n_ka, 8, half), F32),
            pltpu.VMEM((2, 8, half), jnp.int32),
            pltpu.VMEM((2, 8, half), jnp.int32),
            dma((2, 2)),
            dma(()),
            dma((n_half, kblocks)),
            dma((n_half, kblocks)),
            dma((n_half, kblocks)),
            dma((2, n_half, chunks)),
            dma((2, n_half, chunks)),
            dma((2,)),
            dma((2,)),
            dma((2, n_half, chunks)),
            dma((2, n_half, chunks)),
            dma((n_half, parts)),
            dma((n_half, parts)),
            dma((n_half, n_ka)),
            dma((n_half, n_ka)),
            dma((n_half, n_ka)),
            dma((n_half, n_ka)),
            pltpu.SemaphoreType.REGULAR((max(1, n_ka - 3),)),
            pltpu.SemaphoreType.REGULAR((max(1, n_ka - 3),)),
        ],
        compiler_params=pltpu.CompilerParams(
            collective_id=0, has_side_effects=True, vmem_limit_bytes=60 * 2**20
        ),
    )(basis_counts, moments, initial_vectors, final_vectors)
    return amplitude * amplitude


def solution(mesh):
    in_specs = (
        P(None, "vib", None),
        P("ka", "vib", "grp"),
        P("ka", "vib", ("grp", "fin")),
        P(("grp", "ka")),
    )
    out_specs = P(("grp", "ka", "vib"), "fin")
    return jax.shard_map(
        functools.partial(on_device, mesh.shape["ka"]),
        mesh=mesh, in_specs=in_specs, out_specs=out_specs, check_vma=False,
    )
```

```python
import functools

import jax
import jax.numpy as jnp
from jax import lax
from jax.experimental import pallas as pl
from jax.experimental.pallas import tpu as pltpu
from jax.sharding import PartitionSpec as P

JQ = 30
MESH = pl.DeviceIdType.MESH
F32 = jnp.float32
BF16 = jnp.bfloat16
LEVELS = 32767.0
TINY = 1e-30


def coefficient_rows(index, width):
    value = jnp.full((1, width), index, jnp.int32).astype(F32)
    jsquare = float(JQ * (JQ + 1))
    norm_j = jnp.sqrt(jnp.full((1, width), jsquare, F32))
    same = value / norm_j
    upper = 0.5 * jnp.sqrt(jsquare - value * (value + 1.0)) / norm_j
    lower = -0.5 * jnp.sqrt(jsquare - value * (value - 1.0)) / norm_j
    return same, upper, lower


def kernel(
    n_ka, n_half, chunks, groups, counts_hbm, moments_hbm, initial_hbm, final_hbm, out_ref,
    counts, mom, ini, turned, own, edge, comb, split, away, part, zsend, zrecv, ssend, srecv, csend, crecv,
    counts_sem, mom_sem, ini_sem, own_sem, own_send, own_recv, z_send, z_recv, count_send, count_recv,
    fwd_send, fwd_recv, part_send, part_recv, out_send, out_recv, scale_send, scale_recv,
    token_up, token_down,
):
    kblocks, rows, states = ini.shape
    width = final_hbm.shape[2]
    share = out_ref.shape[0]
    whole = mom.shape[2]
    half = width // n_half
    step = rows // chunks
    last = kblocks - 1
    tile = min(256, rows)
    a = lax.axis_index("ka")
    b = lax.axis_index("vib")
    other = 1 - b
    first = a * kblocks - kblocks * n_ka // 2
    cores = (b, other)
    has_up = a < n_ka - 1
    has_down = a > 0
    sends = (has_up, has_down)
    takes = (has_down, has_up)
    toward_side = (a + 1, a - 1)

    barrier = pltpu.get_barrier_semaphore()
    pl.semaphore_signal(barrier, inc=1, device_id={"vib": other}, device_id_type=MESH)
    for side in range(2):
        @pl.when(sends[side])
        def _():
            pl.semaphore_signal(
                barrier, inc=1, device_id={"ka": toward_side[side]}, device_id_type=MESH
            )

    def rows_of(core):
        return pl.ds(pl.multiple_of(core * rows, rows), rows)

    def at(core, j):
        return pl.ds(pl.multiple_of(core * rows + j * step, step), step)

    def half_lanes(i):
        return pl.ds(i * half, half)

    def get_own(h):
        return pltpu.make_async_copy(
            final_hbm.at[:, :, half_lanes(h)], own.at[h, :, rows_of(b)], own_sem.at[h]
        )

    def get_moments(i):
        span = rows_of(cores[i])
        return pltpu.make_async_copy(moments_hbm.at[:, :, span], mom.at[:, :, span], mom_sem.at[i])

    get_counts = pltpu.make_async_copy(counts_hbm, counts, counts_sem)
    get_initial = pltpu.make_async_copy(initial_hbm, ini, ini_sem)

    def own_copy(h):
        return pltpu.make_async_remote_copy(
            src_ref=final_hbm.at[:, :, half_lanes(h)],
            dst_ref=own.at[h, :, rows_of(b)],
            send_sem=own_send.at[h],
            recv_sem=own_recv.at[h],
            device_id={"vib": other},
            device_id_type=MESH,
        )

    def z_copy(side, h, j):
        return pltpu.make_async_remote_copy(
            src_ref=final_hbm.at[last * (1 - side), pl.ds(j * step, step), half_lanes(h)],
            dst_ref=edge.at[h, at(b, j), half_lanes(side)],
            send_sem=z_send.at[side],
            recv_sem=z_recv.at[side, h, j],
            device_id={"ka": toward_side[side]},
            device_id_type=MESH,
        )

    def count_copy(side):
        return pltpu.make_async_remote_copy(
            src_ref=csend.at[side],
            dst_ref=crecv.at[side],
            send_sem=count_send.at[side],
            recv_sem=count_recv.at[side],
            device_id={"ka": toward_side[side]},
            device_id_type=MESH,
        )

    def forward(h, j):
        return pltpu.make_async_remote_copy(
            src_ref=edge.at[h, at(b, j)],
            dst_ref=edge.at[h, at(b, j)],
            send_sem=fwd_send,
            recv_sem=fwd_recv.at[h, j],
            device_id={"vib": other},
            device_id_type=MESH,
        )

    def start_edges(h):
        for j in range(chunks):
            for side in range(2):
                @pl.when(sends[side])
                def _():
                    z_copy(side, h, j).start()

    def start_loads():
        get_counts.start()
        for h in range(n_half):
            get_own(h).start()
        for i in range(2):
            get_moments(i).start()

    def greet():
        for side in range(2):
            @pl.when(jnp.logical_not(takes[side]))
            def _():
                crecv[side] = jnp.zeros(crecv.shape[1:], jnp.int32)
                for h in range(n_half):
                    edge[h, rows_of(b), side * half : (side + 1) * half] = jnp.zeros((rows, half), BF16)
        get_counts.wait()
        for side in range(2):
            csend[side] = jnp.full(csend.shape[1:], counts[last * (1 - side)], jnp.int32)
        pl.semaphore_wait(barrier, 1 + has_up.astype(jnp.int32) + has_down.astype(jnp.int32))
        for side in range(2):
            @pl.when(sends[side])
            def _():
                count_copy(side).start()
        start_edges(0)
        for h in range(n_half):
            own_copy(h).start()

    start_loads()
    greet()

    same0, upper0, _ = coefficient_rows(first, half)
    same1, _, lower1 = coefficient_rows(first + 1, half)
    _, upper_below, _ = coefficient_rows(first - 1, half)
    _, _, lower_above = coefficient_rows(first + 2, half)
    same_row = jnp.concatenate([same0, same1], axis=1)
    cross_row = jnp.concatenate([lower1, upper0], axis=1)
    edge_row = jnp.concatenate([upper_below, lower_above], axis=1)

    rounds = max(0, n_ka - 3)

    def token(side, r):
        sem = (token_up, token_down)[side]
        known = a - 1 - r >= 0 if side == 0 else a + 1 + r <= n_ka - 1

        @pl.when(jnp.logical_and(known, sends[side]))
        def _():
            pl.semaphore_signal(
                sem.at[r - 1], inc=1, device_id={"ka": toward_side[side]}, device_id_type=MESH
            )

    def await_token(side, r):
        sem = (token_up, token_down)[side]

        @pl.when(a - 2 - r >= 0 if side == 0 else a + 2 + r <= n_ka - 1)
        def _():
            pl.semaphore_wait(sem.at[r - 1], 1)

    def relay(h, j):
        for side in range(2):
            @pl.when(takes[side])
            def _():
                z_copy(side, h, j).wait_recv()
        forward(h, j).start()

    def own_half(i, h):
        row_index = lax.broadcasted_iota(jnp.int32, (rows, half), 0) + cores[i] * rows
        if i == 0:
            get_own(h).wait()
        else:
            own_copy(h).wait_recv()
        masked = []
        for k in range(kblocks):
            piece = own[h, k, rows_of(cores[i]), :].astype(F32)
            masked.append(jnp.where(row_index < counts[k], piece, 0.0).astype(BF16))
        piece = jnp.concatenate(masked, axis=1)
        if h == 0:
            get_moments(i).wait()
            if i == 0:
                get_initial.start()
        for t in range(rows // tile):
            span = pl.ds(t * tile, tile)
            along_z = jnp.dot(mom[0, span, rows_of(cores[i])], piece, preferred_element_type=F32)
            along_x = jnp.dot(mom[1, span, rows_of(cores[i])], piece, preferred_element_type=F32)
            crossed = jnp.concatenate([along_x[:, half:], along_x[:, :half]], axis=1)
            value = same_row * along_z + cross_row * crossed
            comb[h, span, :] = value if i == 0 else comb[h, span, :] + value

    def turn_initial():
        get_initial.wait()
        for k in range(kblocks):
            for v in range(rows // tile):
                block = ini[k, v * tile : (v + 1) * tile, :].T
                low = k * rows + v * tile
                for target in range(n_ka):
                    for core in range(2):
                        start = (target * 2 + core) * share
                        turned[core, target * share : (target + 1) * share, low : low + tile] = block[
                            start : start + share
                        ]

    row_index = lax.broadcasted_iota(jnp.int32, (tile, half), 0) + b * rows

    def take(h, core, low, size, last_take=False):
        start = core * rows + low
        edge_index = lax.broadcasted_iota(jnp.int32, (size, 2 * half), 0)
        edge_counts = jnp.concatenate([crecv[0, 0:1, :], crecv[1, 0:1, :]], axis=1)
        span_w = pl.ds(pl.multiple_of(start, size), size)
        piece = edge[h, span_w, :].astype(F32)
        piece = jnp.where(edge_index + start < edge_counts, piece, 0.0).astype(BF16)
        for t in range(rows // tile):
            span = pl.ds(t * tile, tile)
            value = comb[h, span, :] + edge_row * jnp.dot(
                mom[1, span, span_w], piece, preferred_element_type=F32
            )
            if not last_take:
                comb[h, span, :] = value
                continue
            for k in range(kblocks):
                live = jnp.where(
                    row_index + t * tile < counts[k], value[:, k * half : (k + 1) * half], 0.0
                )
                high = live.astype(BF16)
                start_v = k * rows + t * tile
                split[h, start_v : start_v + tile, 0:half] = high
                split[h, start_v : start_v + tile, half:] = (live - high.astype(F32)).astype(BF16)

    targets = n_ka // groups
    size = targets * share

    def part_copy(h, g):
        return pltpu.make_async_remote_copy(
            src_ref=away.at[h, pl.ds(g * size, size)],
            dst_ref=part.at[h, pl.ds(g * size, size)],
            send_sem=part_send,
            recv_sem=part_recv.at[h, g],
            device_id={"vib": other},
            device_id_type=MESH,
        )

    def out_copies(h, sender, target):
        values = pltpu.make_async_remote_copy(
            src_ref=zsend.at[h, target],
            dst_ref=zrecv.at[h, sender],
            send_sem=out_send,
            recv_sem=out_recv.at[h],
            device_id={"ka": target},
            device_id_type=MESH,
        )
        scales = pltpu.make_async_remote_copy(
            src_ref=ssend.at[h, target],
            dst_ref=srecv.at[h, sender],
            send_sem=scale_send,
            recv_sem=scale_recv.at[h],
            device_id={"ka": target},
            device_id_type=MESH,
        )
        return values, scales

    def amplitude(h, core, g):
        both = jnp.dot(
            turned[core, g * size : (g + 1) * size, :], split[h], preferred_element_type=F32
        )
        return both[:, :half] + both[:, half:]

    def send_away(h, g):
        away[h, g * size : (g + 1) * size, :] = amplitude(h, other, g)
        part_copy(h, g).start()

    def finish(h, g):
        mine = amplitude(h, b, g)
        part_copy(h, g).wait_recv()
        mine = mine + part[h, g * size : (g + 1) * size, :]
        for j in range(targets):
            target = g * targets + j
            value = mine[j * share : (j + 1) * share]

            @pl.when(target == a)
            def _():
                out_ref[:, half_lanes(h)] = value

            @pl.when(target != a)
            def _():
                peak = jnp.maximum(jnp.max(jnp.abs(value), axis=0, keepdims=True), TINY)
                zsend[h, target] = jnp.round(value * (LEVELS / peak)).astype(jnp.int16)
                ssend[h, target] = jnp.broadcast_to(peak / LEVELS, (8, half))
                for copy in out_copies(h, a, target):
                    copy.start()

    def all_out(ref, h, send_sem, recv_sem):
        span = ref.at[h, pl.ds(0, n_ka - 1)]
        return pltpu.make_async_remote_copy(
            src_ref=span, dst_ref=span, send_sem=send_sem, recv_sem=recv_sem,
            device_id={"vib": other}, device_id_type=MESH,
        )

    def add_sums(h):
        all_out(zrecv, h, out_send, out_recv.at[h]).wait_recv()
        all_out(srecv, h, scale_send, scale_recv.at[h]).wait_recv()
        total = out_ref[:, half_lanes(h)]
        for d in range(1, n_ka):
            sender = lax.rem(a + d, n_ka)
            total = total + zrecv[h, sender].astype(F32) * srecv[h, sender, 0:1, :]
        out_ref[:, half_lanes(h)] = total

    own_half(0, 0)
    if n_half > 1:
        own_half(0, 1)
    own_half(1, 0)
    for h in range(1, n_half):
        start_edges(h)
    if n_half > 1:
        own_half(1, 1)
    for j in range(chunks):
        if j > 0 or chunks == 1:
            turn_initial()
        relay(0, j)
        if j == 0 and rounds > 0:
            for side in range(2):
                token(side, 1)
    for side in range(2):
        @pl.when(takes[side])
        def _():
            count_copy(side).wait_recv()
    for h in range(n_half):
        if h == 0:
            take(h, b, 0, rows)
            for j in range(chunks):
                forward(h, j).wait_recv()
            take(h, other, 0, rows, last_take=True)
            for r in range(1, rounds + 1):
                for side in range(2):
                    if r > 1:
                        token(side, r)
                for side in range(2):
                    await_token(side, r)
        else:
            for j in range(chunks):
                relay(h, j)
                take(h, b, j * step, step)
                if j > 0:
                    forward(h, j - 1).wait_recv()
                    take(h, other, (j - 1) * step, step)
            forward(h, chunks - 1).wait_recv()
            take(h, other, rows - step, step, last_take=True)
        for g in range(groups):
            send_away(h, g)
        for g in range(groups):
            finish(h, g)
    for h in range(n_half):
        add_sums(h)

    def drain():
        for side in range(2):
            @pl.when(sends[side])
            def _():
                count_copy(side).wait_send()
                pltpu.make_async_remote_copy(
                    src_ref=final_hbm.at[0], dst_ref=final_hbm.at[0],
                    send_sem=z_send.at[side], recv_sem=z_recv.at[side, 0, 0],
                    device_id={"vib": other}, device_id_type=MESH,
                ).wait_send()
        for h in range(n_half):
            own_copy(h).wait_send()
            all_out(zsend, h, out_send, out_recv.at[h]).wait_send()
            all_out(ssend, h, scale_send, scale_recv.at[h]).wait_send()
        for buffer, sem in ((edge.at[:, rows_of(b)], fwd_send), (away, part_send)):
            pltpu.make_async_remote_copy(
                src_ref=buffer, dst_ref=buffer, send_sem=sem, recv_sem=sem,
                device_id={"vib": other}, device_id_type=MESH,
            ).wait_send()

    drain()


def on_device(n_ka, moments, initial_vectors, final_vectors, basis_counts):
    kblocks, rows, states = initial_vectors.shape
    width = final_vectors.shape[2]
    whole = moments.shape[2]
    share = states // (2 * n_ka)
    n_half = max(1, width // 128)
    half = width // n_half
    chunks = 2
    groups = 2
    dma = pltpu.SemaphoreType.DMA
    vmem = pltpu.VMEM
    amplitude = pl.pallas_call(
        functools.partial(kernel, n_ka, n_half, chunks, groups),
        out_shape=vmem((share, width), F32),
        in_specs=[pl.BlockSpec(memory_space=pl.ANY)] * 4,
        out_specs=pl.BlockSpec(memory_space=pltpu.VMEM),
        scratch_shapes=[
            pltpu.SMEM((kblocks,), jnp.int32),
            vmem(moments.shape, BF16),
            vmem(initial_vectors.shape, BF16),
            vmem((2, n_ka * share, kblocks * rows), BF16),
            vmem((n_half, kblocks, whole, half), BF16),
            vmem((n_half, whole, 2 * half), BF16),
            vmem((n_half, rows, kblocks * half), F32),
            vmem((n_half, kblocks * rows, 2 * half), BF16),
            vmem((n_half, n_ka * share, half), F32),
            vmem((n_half, n_ka * share, half), F32),
            vmem((n_half, n_ka, share, half), jnp.int16),
            vmem((n_half, n_ka, share, half), jnp.int16),
            vmem((n_half, n_ka, 8, half), F32),
            vmem((n_half, n_ka, 8, half), F32),
            vmem((2, 8, half), jnp.int32),
            vmem((2, 8, half), jnp.int32),
            dma(()),
            dma((2,)),
            dma(()),
            dma((n_half,)),
            dma((n_half,)),
            dma((n_half,)),
            dma((2,)),
            dma((2, n_half, chunks)),
            dma((2,)),
            dma((2,)),
            dma(()),
            dma((n_half, chunks)),
            dma(()),
            dma((n_half, groups)),
            dma(()),
            dma((n_half,)),
            dma(()),
            dma((n_half,)),
            pltpu.SemaphoreType.REGULAR((max(1, n_ka - 3),)),
            pltpu.SemaphoreType.REGULAR((max(1, n_ka - 3),)),
        ],
        compiler_params=pltpu.CompilerParams(
            collective_id=0, has_side_effects=True, vmem_limit_bytes=60 * 2**20
        ),
    )(basis_counts, moments, initial_vectors, final_vectors)
    return amplitude * amplitude


def solution(mesh):
    in_specs = (
        P(None, "vib", None),
        P("ka", "vib", "grp"),
        P("ka", "vib", ("grp", "fin")),
        P(("grp", "ka")),
    )
    out_specs = P(("grp", "ka", "vib"), "fin")
    return jax.shard_map(
        functools.partial(on_device, mesh.shape["ka"]),
        mesh=mesh, in_specs=in_specs, out_specs=out_specs, check_vma=False,
    )
```

```python
import functools
import math

import jax
import jax.numpy as jnp
from jax import lax
from jax.experimental import pallas as pl
from jax.experimental.pallas import tpu as pltpu
from jax.sharding import PartitionSpec as P

JQ = 30
MESH = pl.DeviceIdType.MESH
F32 = jnp.float32
BF16 = jnp.bfloat16
LEVELS = 32767.0
TINY = 1e-30


def coefficient_rows(index, width):
    value = jnp.full((1, width), index, jnp.int32).astype(F32)
    jsquare = float(JQ * (JQ + 1))
    norm_j = jnp.sqrt(jnp.full((1, width), jsquare, F32))
    same = value / norm_j
    upper = 0.5 * jnp.sqrt(jsquare - value * (value + 1.0)) / norm_j
    lower = -0.5 * jnp.sqrt(jsquare - value * (value - 1.0)) / norm_j
    return same, upper, lower


def kernel(
    n_ka, n_half, cuts, groups, counts_hbm, moments_hbm, initial_hbm, final_hbm, out_ref,
    counts, mom, ini, turned, own, edge, comb, split, away, mine, part, zsend, zrecv, ssend, srecv, csend, crecv,
    counts_sem, mom_sem, ini_sem, own_sem, own_send, own_recv, z_send, z_recv, count_send, count_recv,
    fwd_send, fwd_recv, part_send, part_recv, out_send, out_recv, scale_send, scale_recv,
    token_up, token_down,
):
    kblocks, rows, states = ini.shape
    width = final_hbm.shape[2]
    share = out_ref.shape[0]
    whole = mom.shape[2]
    half = width // n_half
    last = kblocks - 1
    tile = min(256, rows)
    a = lax.axis_index("ka")
    b = lax.axis_index("vib")
    other = 1 - b
    first = a * kblocks - kblocks * n_ka // 2
    cores = (b, other)
    has_up = a < n_ka - 1
    has_down = a > 0
    sends = (has_up, has_down)
    takes = (has_down, has_up)
    toward_side = (a + 1, a - 1)

    barrier = pltpu.get_barrier_semaphore()
    pl.semaphore_signal(barrier, inc=1, device_id={"vib": other}, device_id_type=MESH)
    for side in range(2):
        @pl.when(sends[side])
        def _():
            pl.semaphore_signal(
                barrier, inc=1, device_id={"ka": toward_side[side]}, device_id_type=MESH
            )

    def rows_of(core):
        return pl.ds(pl.multiple_of(core * rows, rows), rows)

    def chunk(h, j):
        bounds = cuts[h]
        return bounds[j], bounds[j + 1] - bounds[j]

    def chunks(h):
        return range(len(cuts[h]) - 1)

    def at(core, h, j):
        low, count = chunk(h, j)
        return pl.ds(pl.multiple_of(core * rows + low, math.gcd(rows, low)), count)

    def half_lanes(i):
        return pl.ds(i * half, half)

    def get_own(h):
        return pltpu.make_async_copy(
            final_hbm.at[:, :, half_lanes(h)], own.at[h, :, rows_of(b)], own_sem.at[h]
        )

    def get_moments(i):
        span = rows_of(cores[i])
        return pltpu.make_async_copy(moments_hbm.at[:, :, span], mom.at[:, :, span], mom_sem.at[i])

    get_counts = pltpu.make_async_copy(counts_hbm, counts, counts_sem)
    get_initial = pltpu.make_async_copy(initial_hbm, ini, ini_sem)

    def own_copy(h):
        return pltpu.make_async_remote_copy(
            src_ref=final_hbm.at[:, :, half_lanes(h)],
            dst_ref=own.at[h, :, rows_of(b)],
            send_sem=own_send.at[h],
            recv_sem=own_recv.at[h],
            device_id={"vib": other},
            device_id_type=MESH,
        )

    def z_copy(side, h, j):
        return pltpu.make_async_remote_copy(
            src_ref=final_hbm.at[last * (1 - side), pl.ds(*chunk(h, j)), half_lanes(h)],
            dst_ref=edge.at[h, at(b, h, j), half_lanes(side)],
            send_sem=z_send.at[side],
            recv_sem=z_recv.at[side, h, j],
            device_id={"ka": toward_side[side]},
            device_id_type=MESH,
        )

    def count_copy(side):
        return pltpu.make_async_remote_copy(
            src_ref=csend.at[side],
            dst_ref=crecv.at[side],
            send_sem=count_send.at[side],
            recv_sem=count_recv.at[side],
            device_id={"ka": toward_side[side]},
            device_id_type=MESH,
        )

    def forward(h, j):
        return pltpu.make_async_remote_copy(
            src_ref=edge.at[h, at(b, h, j)],
            dst_ref=edge.at[h, at(b, h, j)],
            send_sem=fwd_send,
            recv_sem=fwd_recv.at[h, j],
            device_id={"vib": other},
            device_id_type=MESH,
        )

    def start_edges(h):
        for j in chunks(h):
            for side in range(2):
                @pl.when(sends[side])
                def _():
                    z_copy(side, h, j).start()

    def start_loads():
        get_counts.start()
        for h in range(n_half):
            get_own(h).start()
        for i in range(2):
            get_moments(i).start()

    def greet():
        for side in range(2):
            @pl.when(jnp.logical_not(takes[side]))
            def _():
                crecv[side] = jnp.zeros(crecv.shape[1:], jnp.int32)
                for h in range(n_half):
                    edge[h, rows_of(b), side * half : (side + 1) * half] = jnp.zeros((rows, half), BF16)
        get_counts.wait()
        for side in range(2):
            csend[side] = jnp.full(csend.shape[1:], counts[last * (1 - side)], jnp.int32)
        pl.semaphore_wait(barrier, 1 + has_up.astype(jnp.int32) + has_down.astype(jnp.int32))
        for side in range(2):
            @pl.when(sends[side])
            def _():
                count_copy(side).start()
        for h in range(n_half):
            start_edges(h)
        for h in range(n_half):
            own_copy(h).start()

    start_loads()
    greet()

    same0, upper0, _ = coefficient_rows(first, half)
    same1, _, lower1 = coefficient_rows(first + 1, half)
    _, upper_below, _ = coefficient_rows(first - 1, half)
    _, _, lower_above = coefficient_rows(first + 2, half)
    same_row = jnp.concatenate([same0, same1], axis=1)
    cross_row = jnp.concatenate([lower1, upper0], axis=1)
    edge_row = jnp.concatenate([upper_below, lower_above], axis=1)

    rounds = max(0, n_ka - 3)

    def token(side, r):
        sem = (token_up, token_down)[side]
        known = a - 1 - r >= 0 if side == 0 else a + 1 + r <= n_ka - 1

        @pl.when(jnp.logical_and(known, sends[side]))
        def _():
            pl.semaphore_signal(
                sem.at[r - 1], inc=1, device_id={"ka": toward_side[side]}, device_id_type=MESH
            )

    def await_token(side, r):
        sem = (token_up, token_down)[side]

        @pl.when(a - 2 - r >= 0 if side == 0 else a + 2 + r <= n_ka - 1)
        def _():
            pl.semaphore_wait(sem.at[r - 1], 1)

    def relay(h, j):
        for side in range(2):
            @pl.when(takes[side])
            def _():
                z_copy(side, h, j).wait_recv()
        forward(h, j).start()

    def own_half(i, h):
        row_index = lax.broadcasted_iota(jnp.int32, (rows, half), 0) + cores[i] * rows
        if i == 0:
            get_own(h).wait()
        else:
            own_copy(h).wait_recv()
        masked = []
        for k in range(kblocks):
            piece = own[h, k, rows_of(cores[i]), :].astype(F32)
            masked.append(jnp.where(row_index < counts[k], piece, 0.0).astype(BF16))
        piece = jnp.concatenate(masked, axis=1)
        if h == 0:
            get_moments(i).wait()
            if i == 0:
                get_initial.start()
        for t in range(rows // tile):
            span = pl.ds(t * tile, tile)
            along_z = jnp.dot(mom[0, span, rows_of(cores[i])], piece, preferred_element_type=F32)
            along_x = jnp.dot(mom[1, span, rows_of(cores[i])], piece, preferred_element_type=F32)
            crossed = jnp.concatenate([along_x[:, half:], along_x[:, :half]], axis=1)
            value = same_row * along_z + cross_row * crossed
            comb[h, span, :] = value if i == 0 else comb[h, span, :] + value

    def turn_initial():
        get_initial.wait()
        for k in range(kblocks):
            for v in range(rows // tile):
                block = ini[k, v * tile : (v + 1) * tile, :].T
                low = k * rows + v * tile
                for target in range(n_ka):
                    for core in range(2):
                        start = (target * 2 + core) * share
                        turned[core, target * share : (target + 1) * share, low : low + tile] = block[
                            start : start + share
                        ]

    row_index = lax.broadcasted_iota(jnp.int32, (tile, half), 0) + b * rows

    def take(h, core, low, size, last_take=False):
        start = core * rows + low
        edge_index = lax.broadcasted_iota(jnp.int32, (size, 2 * half), 0)
        edge_counts = jnp.concatenate([crecv[0, 0:1, :], crecv[1, 0:1, :]], axis=1)
        span_w = pl.ds(pl.multiple_of(start, math.gcd(rows, low)), size)
        piece = edge[h, span_w, :].astype(F32)
        piece = jnp.where(edge_index + start < edge_counts, piece, 0.0).astype(BF16)
        for t in range(rows // tile):
            span = pl.ds(t * tile, tile)
            value = comb[h, span, :] + edge_row * jnp.dot(
                mom[1, span, span_w], piece, preferred_element_type=F32
            )
            if not last_take:
                comb[h, span, :] = value
                continue
            for k in range(kblocks):
                live = jnp.where(
                    row_index + t * tile < counts[k], value[:, k * half : (k + 1) * half], 0.0
                )
                high = live.astype(BF16)
                start_v = k * rows + t * tile
                split[h, start_v : start_v + tile, 0:half] = high
                split[h, start_v : start_v + tile, half:] = (live - high.astype(F32)).astype(BF16)

    def take_other(h, j):
        forward(h, j).wait_recv()
        take(h, other, *chunk(h, j), last_take=j == len(cuts[h]) - 2)

    targets = n_ka // groups
    size = targets * share

    def part_copy(h, g):
        return pltpu.make_async_remote_copy(
            src_ref=away.at[h, pl.ds(g * size, size)],
            dst_ref=part.at[h, pl.ds(g * size, size)],
            send_sem=part_send,
            recv_sem=part_recv.at[h, g],
            device_id={"vib": other},
            device_id_type=MESH,
        )

    def out_copies(h, sender, target):
        values = pltpu.make_async_remote_copy(
            src_ref=zsend.at[h, target],
            dst_ref=zrecv.at[h, sender],
            send_sem=out_send,
            recv_sem=out_recv.at[h],
            device_id={"ka": target},
            device_id_type=MESH,
        )
        scales = pltpu.make_async_remote_copy(
            src_ref=ssend.at[h, target],
            dst_ref=srecv.at[h, sender],
            send_sem=scale_send,
            recv_sem=scale_recv.at[h],
            device_id={"ka": target},
            device_id_type=MESH,
        )
        return values, scales

    def amplitude(h, core):
        parts = []
        for g in range(groups):
            both = jnp.dot(
                turned[core, g * size : (g + 1) * size, :], split[h], preferred_element_type=F32
            )
            parts.append(both[:, :half] + both[:, half:])
        return parts

    def send_away(h):
        for g, value in enumerate(amplitude(h, other)):
            away[h, g * size : (g + 1) * size, :] = value
        for g in range(groups):
            part_copy(h, g).start()

    def stay(h):
        for g, value in enumerate(amplitude(h, b)):
            mine[g * size : (g + 1) * size, :] = value

    upper_half = (2 * a) // n_ka

    def finish(h):
        for g in range(groups):
            part_copy(h, g).wait_recv()
        for i in range(n_ka):
            target = upper_half * i + (1 - upper_half) * (n_ka - 1 - i)
            span = pl.ds(pl.multiple_of(target * share, share), share)
            value = mine[span, :] + part[h, span, :]

            @pl.when(target == a)
            def _():
                out_ref[:, half_lanes(h)] = value

            @pl.when(target != a)
            def _():
                peak = jnp.maximum(jnp.max(jnp.abs(value), axis=0, keepdims=True), TINY)
                zsend[h, target] = jnp.round(value * (LEVELS / peak)).astype(jnp.int16)
                ssend[h, target] = peak / LEVELS
                for copy in out_copies(h, a, target):
                    copy.start()

    def all_out(ref, h, send_sem, recv_sem):
        span = ref.at[h, pl.ds(0, n_ka - 1)]
        return pltpu.make_async_remote_copy(
            src_ref=span, dst_ref=span, send_sem=send_sem, recv_sem=recv_sem,
            device_id={"vib": other}, device_id_type=MESH,
        )

    def add_sums(h):
        all_out(zrecv, h, out_send, out_recv.at[h]).wait_recv()
        all_out(srecv, h, scale_send, scale_recv.at[h]).wait_recv()
        total = out_ref[:, half_lanes(h)]
        for d in range(1, n_ka):
            sender = lax.rem(a + d, n_ka)
            total = total + zrecv[h, sender].astype(F32) * srecv[h, sender]
        out_ref[:, half_lanes(h)] = total

    own_half(0, 0)
    if n_half > 1:
        own_half(0, 1)
    own_half(1, 0)
    if n_half > 1:
        own_half(1, 1)
    for j in chunks(0):
        if j == len(cuts[0]) - 2:
            turn_initial()
        relay(0, j)
        if j == 0 and rounds > 0:
            for side in range(2):
                token(side, 1)
    for side in range(2):
        @pl.when(takes[side])
        def _():
            count_copy(side).wait_recv()
    for h in range(n_half):
        if h == 0:
            take(h, b, 0, rows)
            for j in chunks(h):
                forward(h, j).wait_recv()
            take(h, other, 0, rows, last_take=True)
            for r in range(1, rounds + 1):
                for side in range(2):
                    if r > 1:
                        token(side, r)
                for side in range(2):
                    await_token(side, r)
        else:
            for j in chunks(h):
                relay(h, j)
                take(h, b, *chunk(h, j))
                if j > 1:
                    take_other(h, j - 2)
            for j in list(chunks(h))[-2:]:
                take_other(h, j)
        send_away(h)
        stay(h)
        finish(h)
    for h in range(n_half):
        add_sums(h)

    def drain():
        for side in range(2):
            @pl.when(sends[side])
            def _():
                count_copy(side).wait_send()
                pltpu.make_async_remote_copy(
                    src_ref=final_hbm.at[0], dst_ref=final_hbm.at[0],
                    send_sem=z_send.at[side], recv_sem=z_recv.at[side, 0, 0],
                    device_id={"vib": other}, device_id_type=MESH,
                ).wait_send()
        for h in range(n_half):
            own_copy(h).wait_send()
            all_out(zsend, h, out_send, out_recv.at[h]).wait_send()
            all_out(ssend, h, scale_send, scale_recv.at[h]).wait_send()
        for buffer, sem in ((edge.at[:, rows_of(b)], fwd_send), (away, part_send)):
            pltpu.make_async_remote_copy(
                src_ref=buffer, dst_ref=buffer, send_sem=sem, recv_sem=sem,
                device_id={"vib": other}, device_id_type=MESH,
            ).wait_send()

    drain()


def on_device(n_ka, moments, initial_vectors, final_vectors, basis_counts):
    kblocks, rows, states = initial_vectors.shape
    width = final_vectors.shape[2]
    whole = moments.shape[2]
    share = states // (2 * n_ka)
    n_half = max(1, width // 128)
    half = width // n_half
    cuts = [[0, rows // 2, rows]] * n_half
    most = max(len(c) for c in cuts) - 1
    groups = 2
    dma = pltpu.SemaphoreType.DMA
    vmem = pltpu.VMEM
    amplitude = pl.pallas_call(
        functools.partial(kernel, n_ka, n_half, cuts, groups),
        out_shape=vmem((share, width), F32),
        in_specs=[pl.BlockSpec(memory_space=pl.ANY)] * 4,
        out_specs=pl.BlockSpec(memory_space=pltpu.VMEM),
        scratch_shapes=[
            pltpu.SMEM((kblocks,), jnp.int32),
            vmem(moments.shape, BF16),
            vmem(initial_vectors.shape, BF16),
            vmem((2, n_ka * share, kblocks * rows), BF16),
            vmem((n_half, kblocks, whole, half), BF16),
            vmem((n_half, whole, 2 * half), BF16),
            vmem((n_half, rows, kblocks * half), F32),
            vmem((n_half, kblocks * rows, 2 * half), BF16),
            vmem((n_half, n_ka * share, half), F32),
            vmem((n_ka * share, half), F32),
            vmem((n_half, n_ka * share, half), F32),
            vmem((n_half, n_ka, share, half), jnp.int16),
            vmem((n_half, n_ka, share, half), jnp.int16),
            vmem((n_half, n_ka, 1, half), F32),
            vmem((n_half, n_ka, 1, half), F32),
            vmem((2, 8, half), jnp.int32),
            vmem((2, 8, half), jnp.int32),
            dma(()),
            dma((2,)),
            dma(()),
            dma((n_half,)),
            dma((n_half,)),
            dma((n_half,)),
            dma((2,)),
            dma((2, n_half, most)),
            dma((2,)),
            dma((2,)),
            dma(()),
            dma((n_half, most)),
            dma(()),
            dma((n_half, groups)),
            dma(()),
            dma((n_half,)),
            dma(()),
            dma((n_half,)),
            pltpu.SemaphoreType.REGULAR((max(1, n_ka - 3),)),
            pltpu.SemaphoreType.REGULAR((max(1, n_ka - 3),)),
        ],
        compiler_params=pltpu.CompilerParams(
            collective_id=0, has_side_effects=True, vmem_limit_bytes=60 * 2**20
        ),
    )(basis_counts, moments, initial_vectors, final_vectors)
    return amplitude * amplitude


def solution(mesh):
    in_specs = (
        P(None, "vib", None),
        P("ka", "vib", "grp"),
        P("ka", "vib", ("grp", "fin")),
        P(("grp", "ka")),
    )
    out_specs = P(("grp", "ka", "vib"), "fin")
    return jax.shard_map(
        functools.partial(on_device, mesh.shape["ka"]),
        mesh=mesh, in_specs=in_specs, out_specs=out_specs, check_vma=False,
    )
```

```python
import functools
import math

import jax
import jax.numpy as jnp
from jax import lax
from jax.experimental import pallas as pl
from jax.experimental.pallas import tpu as pltpu
from jax.sharding import PartitionSpec as P

JQ = 30
MESH = pl.DeviceIdType.MESH
F32 = jnp.float32
BF16 = jnp.bfloat16
LEVELS = 32767.0
TINY = 1e-30


def coefficient_rows(index, width):
    value = jnp.full((1, width), index, jnp.int32).astype(F32)
    jsquare = float(JQ * (JQ + 1))
    norm_j = jnp.sqrt(jnp.full((1, width), jsquare, F32))
    same = value / norm_j
    upper = 0.5 * jnp.sqrt(jsquare - value * (value + 1.0)) / norm_j
    lower = -0.5 * jnp.sqrt(jsquare - value * (value - 1.0)) / norm_j
    return same, upper, lower


def kernel(
    n_ka, n_half, cuts, groups, counts_hbm, moments_hbm, initial_hbm, final_hbm, out_ref,
    counts, mom, ini, turned, own, edge, comb, split, away, mine, part, zsend, zrecv, ssend, srecv, csend, crecv,
    counts_sem, mom_sem, ini_sem, own_sem, own_send, own_recv, z_send, z_recv, count_send, count_recv,
    fwd_send, fwd_recv, part_send, part_recv, out_send, out_recv, scale_send, scale_recv,
    token_up, token_down,
):
    kblocks, rows, states = ini.shape
    width = final_hbm.shape[2]
    share = out_ref.shape[0]
    whole = mom.shape[2]
    half = width // n_half
    last = kblocks - 1
    tile = min(256, rows)
    a = lax.axis_index("ka")
    b = lax.axis_index("vib")
    other = 1 - b
    first = a * kblocks - kblocks * n_ka // 2
    cores = (b, other)
    has_up = a < n_ka - 1
    has_down = a > 0
    sends = (has_up, has_down)
    takes = (has_down, has_up)
    toward_side = (a + 1, a - 1)

    barrier = pltpu.get_barrier_semaphore()
    pl.semaphore_signal(barrier, inc=1, device_id={"vib": other}, device_id_type=MESH)
    for side in range(2):
        @pl.when(sends[side])
        def _():
            pl.semaphore_signal(
                barrier, inc=1, device_id={"ka": toward_side[side]}, device_id_type=MESH
            )

    def rows_of(core):
        return pl.ds(pl.multiple_of(core * rows, rows), rows)

    def chunk(h, j):
        bounds = cuts[h]
        return bounds[j], bounds[j + 1] - bounds[j]

    def chunks(h):
        return range(len(cuts[h]) - 1)

    def at(core, h, j):
        low, count = chunk(h, j)
        return pl.ds(pl.multiple_of(core * rows + low, math.gcd(rows, low)), count)

    def half_lanes(i):
        return pl.ds(i * half, half)

    def get_own(h):
        return pltpu.make_async_copy(
            final_hbm.at[:, :, half_lanes(h)], own.at[h, :, rows_of(b)], own_sem.at[h]
        )

    def get_moments(i):
        span = rows_of(cores[i])
        return pltpu.make_async_copy(moments_hbm.at[:, :, span], mom.at[:, :, span], mom_sem.at[i])

    get_counts = pltpu.make_async_copy(counts_hbm, counts, counts_sem)
    get_initial = pltpu.make_async_copy(initial_hbm, ini, ini_sem)

    def own_copy(h):
        return pltpu.make_async_remote_copy(
            src_ref=final_hbm.at[:, :, half_lanes(h)],
            dst_ref=own.at[h, :, rows_of(b)],
            send_sem=own_send.at[h],
            recv_sem=own_recv.at[h],
            device_id={"vib": other},
            device_id_type=MESH,
        )

    def z_copy(side, h, j):
        return pltpu.make_async_remote_copy(
            src_ref=final_hbm.at[last * (1 - side), pl.ds(*chunk(h, j)), half_lanes(h)],
            dst_ref=edge.at[h, at(b, h, j), half_lanes(side)],
            send_sem=z_send.at[side],
            recv_sem=z_recv.at[side, h, j],
            device_id={"ka": toward_side[side]},
            device_id_type=MESH,
        )

    def count_copy(side):
        return pltpu.make_async_remote_copy(
            src_ref=csend.at[side],
            dst_ref=crecv.at[side],
            send_sem=count_send.at[side],
            recv_sem=count_recv.at[side],
            device_id={"ka": toward_side[side]},
            device_id_type=MESH,
        )

    def forward(h, j):
        return pltpu.make_async_remote_copy(
            src_ref=edge.at[h, at(b, h, j)],
            dst_ref=edge.at[h, at(b, h, j)],
            send_sem=fwd_send,
            recv_sem=fwd_recv.at[h, j],
            device_id={"vib": other},
            device_id_type=MESH,
        )

    def start_edges(h):
        for j in chunks(h):
            for side in range(2):
                @pl.when(sends[side])
                def _():
                    z_copy(side, h, j).start()

    def start_loads():
        get_counts.start()
        for h in range(n_half):
            get_own(h).start()
        for i in range(2):
            get_moments(i).start()

    def greet():
        for side in range(2):
            @pl.when(jnp.logical_not(takes[side]))
            def _():
                crecv[side] = jnp.zeros(crecv.shape[1:], jnp.int32)
                for h in range(n_half):
                    edge[h, rows_of(b), side * half : (side + 1) * half] = jnp.zeros((rows, half), BF16)
        get_counts.wait()
        for side in range(2):
            csend[side] = jnp.full(csend.shape[1:], counts[last * (1 - side)], jnp.int32)
        pl.semaphore_wait(barrier, 1 + has_up.astype(jnp.int32) + has_down.astype(jnp.int32))
        for side in range(2):
            @pl.when(sends[side])
            def _():
                count_copy(side).start()
        start_edges(0)
        for h in range(n_half):
            own_copy(h).start()

        @pl.when(b == 0)
        def _():
            for h in range(1, n_half):
                start_edges(h)

    start_loads()
    greet()

    same0, upper0, _ = coefficient_rows(first, half)
    same1, _, lower1 = coefficient_rows(first + 1, half)
    _, upper_below, _ = coefficient_rows(first - 1, half)
    _, _, lower_above = coefficient_rows(first + 2, half)
    same_row = jnp.concatenate([same0, same1], axis=1)
    cross_row = jnp.concatenate([lower1, upper0], axis=1)
    edge_row = jnp.concatenate([upper_below, lower_above], axis=1)

    rounds = max(0, n_ka - 3)

    def token(side, r):
        sem = (token_up, token_down)[side]
        known = a - 1 - r >= 0 if side == 0 else a + 1 + r <= n_ka - 1

        @pl.when(jnp.logical_and(known, sends[side]))
        def _():
            pl.semaphore_signal(
                sem.at[r - 1], inc=1, device_id={"ka": toward_side[side]}, device_id_type=MESH
            )

    def await_token(side, r):
        sem = (token_up, token_down)[side]

        @pl.when(a - 2 - r >= 0 if side == 0 else a + 2 + r <= n_ka - 1)
        def _():
            pl.semaphore_wait(sem.at[r - 1], 1)

    def relay(h, j):
        for side in range(2):
            @pl.when(takes[side])
            def _():
                z_copy(side, h, j).wait_recv()
        forward(h, j).start()

    def own_half(i, h):
        row_index = lax.broadcasted_iota(jnp.int32, (rows, half), 0) + cores[i] * rows
        if i == 0:
            get_own(h).wait()
        else:
            own_copy(h).wait_recv()
        masked = []
        for k in range(kblocks):
            piece = own[h, k, rows_of(cores[i]), :].astype(F32)
            masked.append(jnp.where(row_index < counts[k], piece, 0.0).astype(BF16))
        piece = jnp.concatenate(masked, axis=1)
        if h == 0:
            get_moments(i).wait()
            if i == 0:
                get_initial.start()
        for t in range(rows // tile):
            span = pl.ds(t * tile, tile)
            along_z = jnp.dot(mom[0, span, rows_of(cores[i])], piece, preferred_element_type=F32)
            along_x = jnp.dot(mom[1, span, rows_of(cores[i])], piece, preferred_element_type=F32)
            crossed = jnp.concatenate([along_x[:, half:], along_x[:, :half]], axis=1)
            value = same_row * along_z + cross_row * crossed
            comb[h, span, :] = value if i == 0 else comb[h, span, :] + value

    def turn_initial():
        get_initial.wait()
        for k in range(kblocks):
            for v in range(rows // tile):
                block = ini[k, v * tile : (v + 1) * tile, :].T
                low = k * rows + v * tile
                for target in range(n_ka):
                    for core in range(2):
                        start = (target * 2 + core) * share
                        turned[core, target * share : (target + 1) * share, low : low + tile] = block[
                            start : start + share
                        ]

    row_index = lax.broadcasted_iota(jnp.int32, (tile, half), 0) + b * rows

    def take(h, core, low, size, last_take=False):
        start = core * rows + low
        edge_index = lax.broadcasted_iota(jnp.int32, (size, 2 * half), 0)
        edge_counts = jnp.concatenate([crecv[0, 0:1, :], crecv[1, 0:1, :]], axis=1)
        span_w = pl.ds(pl.multiple_of(start, math.gcd(rows, low)), size)
        piece = edge[h, span_w, :].astype(F32)
        piece = jnp.where(edge_index + start < edge_counts, piece, 0.0).astype(BF16)
        for t in range(rows // tile):
            span = pl.ds(t * tile, tile)
            value = comb[h, span, :] + edge_row * jnp.dot(
                mom[1, span, span_w], piece, preferred_element_type=F32
            )
            if not last_take:
                comb[h, span, :] = value
                continue
            for k in range(kblocks):
                live = jnp.where(
                    row_index + t * tile < counts[k], value[:, k * half : (k + 1) * half], 0.0
                )
                high = live.astype(BF16)
                start_v = k * rows + t * tile
                split[h, start_v : start_v + tile, 0:half] = high
                split[h, start_v : start_v + tile, half:] = (live - high.astype(F32)).astype(BF16)

    def take_other(h, j):
        forward(h, j).wait_recv()
        take(h, other, *chunk(h, j), last_take=j == len(cuts[h]) - 2)

    targets = n_ka // groups
    size = targets * share

    def part_copy(h, g):
        return pltpu.make_async_remote_copy(
            src_ref=away.at[h, pl.ds(g * size, size)],
            dst_ref=part.at[h, pl.ds(g * size, size)],
            send_sem=part_send,
            recv_sem=part_recv.at[h, g],
            device_id={"vib": other},
            device_id_type=MESH,
        )

    def out_copies(h, sender, target):
        values = pltpu.make_async_remote_copy(
            src_ref=zsend.at[h, target],
            dst_ref=zrecv.at[h, sender],
            send_sem=out_send,
            recv_sem=out_recv.at[h],
            device_id={"ka": target},
            device_id_type=MESH,
        )
        scales = pltpu.make_async_remote_copy(
            src_ref=ssend.at[h, target],
            dst_ref=srecv.at[h, sender],
            send_sem=scale_send,
            recv_sem=scale_recv.at[h],
            device_id={"ka": target},
            device_id_type=MESH,
        )
        return values, scales

    def amplitude(h, core):
        parts = []
        for g in range(groups):
            both = jnp.dot(
                turned[core, g * size : (g + 1) * size, :], split[h], preferred_element_type=F32
            )
            parts.append(both[:, :half] + both[:, half:])
        return parts

    def send_away(h):
        for g, value in enumerate(amplitude(h, other)):
            away[h, g * size : (g + 1) * size, :] = value
        for g in range(groups):
            part_copy(h, g).start()

    def stay(h):
        for g, value in enumerate(amplitude(h, b)):
            mine[g * size : (g + 1) * size, :] = value

    upper_half = (2 * a) // n_ka

    def finish(h):
        for g in range(groups):
            part_copy(h, g).wait_recv()
        for i in range(n_ka):
            target = upper_half * i + (1 - upper_half) * (n_ka - 1 - i)
            span = pl.ds(pl.multiple_of(target * share, share), share)
            value = mine[span, :] + part[h, span, :]

            @pl.when(target == a)
            def _():
                out_ref[:, half_lanes(h)] = value

            @pl.when(target != a)
            def _():
                peak = jnp.maximum(jnp.max(jnp.abs(value), axis=0, keepdims=True), TINY)
                zsend[h, target] = jnp.round(value * (LEVELS / peak)).astype(jnp.int16)
                ssend[h, target] = peak / LEVELS
                for copy in out_copies(h, a, target):
                    copy.start()

    def all_out(ref, h, send_sem, recv_sem):
        span = ref.at[h, pl.ds(0, n_ka - 1)]
        return pltpu.make_async_remote_copy(
            src_ref=span, dst_ref=span, send_sem=send_sem, recv_sem=recv_sem,
            device_id={"vib": other}, device_id_type=MESH,
        )

    def add_sums(h):
        all_out(zrecv, h, out_send, out_recv.at[h]).wait_recv()
        all_out(srecv, h, scale_send, scale_recv.at[h]).wait_recv()
        total = out_ref[:, half_lanes(h)]
        for d in range(1, n_ka):
            sender = lax.rem(a + d, n_ka)
            total = total + zrecv[h, sender].astype(F32) * srecv[h, sender]
        out_ref[:, half_lanes(h)] = total

    own_half(0, 0)
    if n_half > 1:
        own_half(0, 1)
    own_half(1, 0)
    if n_half > 1:
        own_half(1, 1)
    for j in chunks(0):
        if j == len(cuts[0]) - 2:
            turn_initial()

            @pl.when(b == 1)
            def _():
                for h in range(1, n_half):
                    start_edges(h)
        relay(0, j)
        if j == 0 and rounds > 0:
            for side in range(2):
                token(side, 1)
    for side in range(2):
        @pl.when(takes[side])
        def _():
            count_copy(side).wait_recv()
    for h in range(n_half):
        if h == 0:
            take(h, b, 0, rows)
            for j in chunks(h):
                forward(h, j).wait_recv()
            take(h, other, 0, rows, last_take=True)
            for r in range(1, rounds + 1):
                for side in range(2):
                    if r > 1:
                        token(side, r)
                for side in range(2):
                    await_token(side, r)
        else:
            for j in chunks(h):
                relay(h, j)
                take(h, b, *chunk(h, j))
                if j > 1:
                    take_other(h, j - 2)
            for j in list(chunks(h))[-2:]:
                take_other(h, j)
        send_away(h)
        stay(h)
        finish(h)
    for h in range(n_half):
        add_sums(h)

    def drain():
        for side in range(2):
            @pl.when(sends[side])
            def _():
                count_copy(side).wait_send()
                pltpu.make_async_remote_copy(
                    src_ref=final_hbm.at[0], dst_ref=final_hbm.at[0],
                    send_sem=z_send.at[side], recv_sem=z_recv.at[side, 0, 0],
                    device_id={"vib": other}, device_id_type=MESH,
                ).wait_send()
        for h in range(n_half):
            own_copy(h).wait_send()
            all_out(zsend, h, out_send, out_recv.at[h]).wait_send()
            all_out(ssend, h, scale_send, scale_recv.at[h]).wait_send()
        for buffer, sem in ((edge.at[:, rows_of(b)], fwd_send), (away, part_send)):
            pltpu.make_async_remote_copy(
                src_ref=buffer, dst_ref=buffer, send_sem=sem, recv_sem=sem,
                device_id={"vib": other}, device_id_type=MESH,
            ).wait_send()

    drain()


def on_device(n_ka, moments, initial_vectors, final_vectors, basis_counts):
    kblocks, rows, states = initial_vectors.shape
    width = final_vectors.shape[2]
    whole = moments.shape[2]
    share = states // (2 * n_ka)
    n_half = max(1, width // 128)
    half = width // n_half
    cuts = [[0, rows // 2, rows]] * n_half
    most = max(len(c) for c in cuts) - 1
    groups = 2
    dma = pltpu.SemaphoreType.DMA
    vmem = pltpu.VMEM
    amplitude = pl.pallas_call(
        functools.partial(kernel, n_ka, n_half, cuts, groups),
        out_shape=vmem((share, width), F32),
        in_specs=[pl.BlockSpec(memory_space=pl.ANY)] * 4,
        out_specs=pl.BlockSpec(memory_space=pltpu.VMEM),
        scratch_shapes=[
            pltpu.SMEM((kblocks,), jnp.int32),
            vmem(moments.shape, BF16),
            vmem(initial_vectors.shape, BF16),
            vmem((2, n_ka * share, kblocks * rows), BF16),
            vmem((n_half, kblocks, whole, half), BF16),
            vmem((n_half, whole, 2 * half), BF16),
            vmem((n_half, rows, kblocks * half), F32),
            vmem((n_half, kblocks * rows, 2 * half), BF16),
            vmem((n_half, n_ka * share, half), F32),
            vmem((n_ka * share, half), F32),
            vmem((n_half, n_ka * share, half), F32),
            vmem((n_half, n_ka, share, half), jnp.int16),
            vmem((n_half, n_ka, share, half), jnp.int16),
            vmem((n_half, n_ka, 1, half), F32),
            vmem((n_half, n_ka, 1, half), F32),
            vmem((2, 8, half), jnp.int32),
            vmem((2, 8, half), jnp.int32),
            dma(()),
            dma((2,)),
            dma(()),
            dma((n_half,)),
            dma((n_half,)),
            dma((n_half,)),
            dma((2,)),
            dma((2, n_half, most)),
            dma((2,)),
            dma((2,)),
            dma(()),
            dma((n_half, most)),
            dma(()),
            dma((n_half, groups)),
            dma(()),
            dma((n_half,)),
            dma(()),
            dma((n_half,)),
            pltpu.SemaphoreType.REGULAR((max(1, n_ka - 3),)),
            pltpu.SemaphoreType.REGULAR((max(1, n_ka - 3),)),
        ],
        compiler_params=pltpu.CompilerParams(
            collective_id=0, has_side_effects=True, vmem_limit_bytes=60 * 2**20
        ),
    )(basis_counts, moments, initial_vectors, final_vectors)
    return amplitude * amplitude


def solution(mesh):
    in_specs = (
        P(None, "vib", None),
        P("ka", "vib", "grp"),
        P("ka", "vib", ("grp", "fin")),
        P(("grp", "ka")),
    )
    out_specs = P(("grp", "ka", "vib"), "fin")
    return jax.shard_map(
        functools.partial(on_device, mesh.shape["ka"]),
        mesh=mesh, in_specs=in_specs, out_specs=out_specs, check_vma=False,
    )
```

```python
import functools
import math

import jax
import jax.numpy as jnp
from jax import lax
from jax.experimental import pallas as pl
from jax.experimental.pallas import tpu as pltpu
from jax.sharding import PartitionSpec as P

JQ = 30
MESH = pl.DeviceIdType.MESH
F32 = jnp.float32
BF16 = jnp.bfloat16
LEVELS = 32767.0
TINY = 1e-30


def coefficient_rows(index, width):
    value = jnp.full((1, width), index, jnp.int32).astype(F32)
    jsquare = float(JQ * (JQ + 1))
    norm_j = jnp.sqrt(jnp.full((1, width), jsquare, F32))
    same = value / norm_j
    upper = 0.5 * jnp.sqrt(jsquare - value * (value + 1.0)) / norm_j
    lower = -0.5 * jnp.sqrt(jsquare - value * (value - 1.0)) / norm_j
    return same, upper, lower


def kernel(
    n_ka, n_half, cuts, groups, counts_hbm, moments_hbm, initial_hbm, final_hbm, out_ref,
    counts, mom, ini, turned, own, edge, comb, split, away, away_scale, mine, part, part_scale, zsend, zrecv, ssend, srecv, csend, crecv,
    counts_sem, mom_sem, ini_sem, own_sem, own_send, own_recv, z_send, z_recv, count_send, count_recv,
    fwd_send, fwd_recv, part_send, part_recv, part_scale_send, part_scale_recv, out_send, out_recv, scale_send, scale_recv,
    token_up, token_down,
):
    kblocks, rows, states = ini.shape
    width = final_hbm.shape[2]
    share = out_ref.shape[0]
    whole = mom.shape[2]
    half = width // n_half
    last = kblocks - 1
    tile = min(256, rows)
    a = lax.axis_index("ka")
    b = lax.axis_index("vib")
    other = 1 - b
    first = a * kblocks - kblocks * n_ka // 2
    cores = (b, other)
    has_up = a < n_ka - 1
    has_down = a > 0
    sends = (has_up, has_down)
    takes = (has_down, has_up)
    toward_side = (a + 1, a - 1)

    barrier = pltpu.get_barrier_semaphore()
    pl.semaphore_signal(barrier, inc=1, device_id={"vib": other}, device_id_type=MESH)
    for side in range(2):
        @pl.when(sends[side])
        def _():
            pl.semaphore_signal(
                barrier, inc=1, device_id={"ka": toward_side[side]}, device_id_type=MESH
            )

    def rows_of(core):
        return pl.ds(pl.multiple_of(core * rows, rows), rows)

    def chunk(h, j):
        bounds = cuts[h]
        return bounds[j], bounds[j + 1] - bounds[j]

    def chunks(h):
        return range(len(cuts[h]) - 1)

    def at(core, h, j):
        low, count = chunk(h, j)
        return pl.ds(pl.multiple_of(core * rows + low, math.gcd(rows, low)), count)

    def half_lanes(i):
        return pl.ds(i * half, half)

    def get_own(h):
        return pltpu.make_async_copy(
            final_hbm.at[:, :, half_lanes(h)], own.at[h, :, rows_of(b)], own_sem.at[h]
        )

    def get_moments(i):
        span = rows_of(cores[i])
        return pltpu.make_async_copy(moments_hbm.at[:, :, span], mom.at[:, :, span], mom_sem.at[i])

    get_counts = pltpu.make_async_copy(counts_hbm, counts, counts_sem)
    get_initial = pltpu.make_async_copy(initial_hbm, ini, ini_sem)

    def own_copy(h):
        return pltpu.make_async_remote_copy(
            src_ref=final_hbm.at[:, :, half_lanes(h)],
            dst_ref=own.at[h, :, rows_of(b)],
            send_sem=own_send.at[h],
            recv_sem=own_recv.at[h],
            device_id={"vib": other},
            device_id_type=MESH,
        )

    def z_copy(side, h, j):
        return pltpu.make_async_remote_copy(
            src_ref=final_hbm.at[last * (1 - side), pl.ds(*chunk(h, j)), half_lanes(h)],
            dst_ref=edge.at[h, at(b, h, j), half_lanes(side)],
            send_sem=z_send.at[side],
            recv_sem=z_recv.at[side, h, j],
            device_id={"ka": toward_side[side]},
            device_id_type=MESH,
        )

    def count_copy(side):
        return pltpu.make_async_remote_copy(
            src_ref=csend.at[side],
            dst_ref=crecv.at[side],
            send_sem=count_send.at[side],
            recv_sem=count_recv.at[side],
            device_id={"ka": toward_side[side]},
            device_id_type=MESH,
        )

    def forward(h, j):
        return pltpu.make_async_remote_copy(
            src_ref=edge.at[h, at(b, h, j)],
            dst_ref=edge.at[h, at(b, h, j)],
            send_sem=fwd_send,
            recv_sem=fwd_recv.at[h, j],
            device_id={"vib": other},
            device_id_type=MESH,
        )

    def start_edges(h):
        for j in chunks(h):
            for side in range(2):
                @pl.when(sends[side])
                def _():
                    z_copy(side, h, j).start()

    def start_loads():
        get_counts.start()
        for h in range(n_half):
            get_own(h).start()
        for i in range(2):
            get_moments(i).start()

    def greet():
        for side in range(2):
            @pl.when(jnp.logical_not(takes[side]))
            def _():
                crecv[side] = jnp.zeros(crecv.shape[1:], jnp.int32)
                for h in range(n_half):
                    edge[h, rows_of(b), side * half : (side + 1) * half] = jnp.zeros((rows, half), BF16)
        get_counts.wait()
        for side in range(2):
            csend[side] = jnp.full(csend.shape[1:], counts[last * (1 - side)], jnp.int32)
        pl.semaphore_wait(barrier, 1 + has_up.astype(jnp.int32) + has_down.astype(jnp.int32))
        for side in range(2):
            @pl.when(sends[side])
            def _():
                count_copy(side).start()
        start_edges(0)
        for h in range(n_half):
            own_copy(h).start()

        @pl.when(b == 0)
        def _():
            for h in range(1, n_half):
                start_edges(h)

    start_loads()
    greet()

    same0, upper0, _ = coefficient_rows(first, half)
    same1, _, lower1 = coefficient_rows(first + 1, half)
    _, upper_below, _ = coefficient_rows(first - 1, half)
    _, _, lower_above = coefficient_rows(first + 2, half)
    same_row = jnp.concatenate([same0, same1], axis=1)
    cross_row = jnp.concatenate([lower1, upper0], axis=1)
    edge_row = jnp.concatenate([upper_below, lower_above], axis=1)

    rounds = max(0, n_ka - 3)

    def token(side, r):
        sem = (token_up, token_down)[side]
        known = a - 1 - r >= 0 if side == 0 else a + 1 + r <= n_ka - 1

        @pl.when(jnp.logical_and(known, sends[side]))
        def _():
            pl.semaphore_signal(
                sem.at[r - 1], inc=1, device_id={"ka": toward_side[side]}, device_id_type=MESH
            )

    def await_token(side, r):
        sem = (token_up, token_down)[side]

        @pl.when(a - 2 - r >= 0 if side == 0 else a + 2 + r <= n_ka - 1)
        def _():
            pl.semaphore_wait(sem.at[r - 1], 1)

    def relay(h, j):
        for side in range(2):
            @pl.when(takes[side])
            def _():
                z_copy(side, h, j).wait_recv()
        forward(h, j).start()

    def own_half(i, h):
        row_index = lax.broadcasted_iota(jnp.int32, (rows, half), 0) + cores[i] * rows
        if i == 0:
            get_own(h).wait()
        else:
            own_copy(h).wait_recv()
        masked = []
        for k in range(kblocks):
            piece = own[h, k, rows_of(cores[i]), :].astype(F32)
            masked.append(jnp.where(row_index < counts[k], piece, 0.0).astype(BF16))
        piece = jnp.concatenate(masked, axis=1)
        if h == 0:
            get_moments(i).wait()
            if i == 0:
                get_initial.start()
        for t in range(rows // tile):
            span = pl.ds(t * tile, tile)
            along_z = jnp.dot(mom[0, span, rows_of(cores[i])], piece, preferred_element_type=F32)
            along_x = jnp.dot(mom[1, span, rows_of(cores[i])], piece, preferred_element_type=F32)
            crossed = jnp.concatenate([along_x[:, half:], along_x[:, :half]], axis=1)
            value = same_row * along_z + cross_row * crossed
            comb[h, span, :] = value if i == 0 else comb[h, span, :] + value

    def turn_initial():
        get_initial.wait()
        for k in range(kblocks):
            for v in range(rows // tile):
                block = ini[k, v * tile : (v + 1) * tile, :].T
                low = k * rows + v * tile
                for target in range(n_ka):
                    for core in range(2):
                        start = (target * 2 + core) * share
                        turned[core, target * share : (target + 1) * share, low : low + tile] = block[
                            start : start + share
                        ]

    row_index = lax.broadcasted_iota(jnp.int32, (tile, half), 0) + b * rows

    def take(h, core, low, size, last_take=False):
        start = core * rows + low
        edge_index = lax.broadcasted_iota(jnp.int32, (size, 2 * half), 0)
        edge_counts = jnp.concatenate([crecv[0, 0:1, :], crecv[1, 0:1, :]], axis=1)
        span_w = pl.ds(pl.multiple_of(start, math.gcd(rows, low)), size)
        piece = edge[h, span_w, :].astype(F32)
        piece = jnp.where(edge_index + start < edge_counts, piece, 0.0).astype(BF16)
        for t in range(rows // tile):
            span = pl.ds(t * tile, tile)
            value = comb[h, span, :] + edge_row * jnp.dot(
                mom[1, span, span_w], piece, preferred_element_type=F32
            )
            if not last_take:
                comb[h, span, :] = value
                continue
            for k in range(kblocks):
                live = jnp.where(
                    row_index + t * tile < counts[k], value[:, k * half : (k + 1) * half], 0.0
                )
                high = live.astype(BF16)
                start_v = k * rows + t * tile
                split[h, start_v : start_v + tile, 0:half] = high
                split[h, start_v : start_v + tile, half:] = (live - high.astype(F32)).astype(BF16)

    def take_other(h, j):
        forward(h, j).wait_recv()
        take(h, other, *chunk(h, j), last_take=j == len(cuts[h]) - 2)

    targets = n_ka // groups
    size = targets * share

    def part_copies(h):
        values = pltpu.make_async_remote_copy(
            src_ref=away.at[h],
            dst_ref=part.at[h],
            send_sem=part_send,
            recv_sem=part_recv.at[h],
            device_id={"vib": other},
            device_id_type=MESH,
        )
        scales = pltpu.make_async_remote_copy(
            src_ref=away_scale.at[h],
            dst_ref=part_scale.at[h],
            send_sem=part_scale_send,
            recv_sem=part_scale_recv.at[h],
            device_id={"vib": other},
            device_id_type=MESH,
        )
        return values, scales

    def pack(value):
        peak = jnp.maximum(jnp.max(jnp.abs(value), axis=0, keepdims=True), TINY)
        return jnp.round(value * (LEVELS / peak)).astype(jnp.int16), peak / LEVELS

    def out_copies(h, sender, target):
        values = pltpu.make_async_remote_copy(
            src_ref=zsend.at[h, target],
            dst_ref=zrecv.at[h, sender],
            send_sem=out_send,
            recv_sem=out_recv.at[h],
            device_id={"ka": target},
            device_id_type=MESH,
        )
        scales = pltpu.make_async_remote_copy(
            src_ref=ssend.at[h, target],
            dst_ref=srecv.at[h, sender],
            send_sem=scale_send,
            recv_sem=scale_recv.at[h],
            device_id={"ka": target},
            device_id_type=MESH,
        )
        return values, scales

    def amplitude(h, core):
        parts = []
        for g in range(groups):
            both = jnp.dot(
                turned[core, g * size : (g + 1) * size, :], split[h], preferred_element_type=F32
            )
            parts.append(both[:, :half] + both[:, half:])
        return parts

    def send_away(h):
        for g, value in enumerate(amplitude(h, other)):
            away[h, g * size : (g + 1) * size, :], away_scale[h, g] = pack(value)
        for copy in part_copies(h):
            copy.start()

    def stay(h):
        for g, value in enumerate(amplitude(h, b)):
            mine[g * size : (g + 1) * size, :] = value
        for copy in part_copies(h):
            copy.wait_recv()
        for g in range(groups):
            span = pl.ds(g * size, size)
            mine[span, :] = mine[span, :] + part[h, span, :].astype(F32) * part_scale[h, g]

    upper_half = (2 * a) // n_ka

    def finish(h):
        for i in range(n_ka):
            target = upper_half * i + (1 - upper_half) * (n_ka - 1 - i)
            span = pl.ds(pl.multiple_of(target * share, share), share)
            value = mine[span, :]

            @pl.when(target == a)
            def _():
                out_ref[:, half_lanes(h)] = value

            @pl.when(target != a)
            def _():
                zsend[h, target], ssend[h, target] = pack(value)
                for copy in out_copies(h, a, target):
                    copy.start()

    def all_out(ref, h, send_sem, recv_sem):
        span = ref.at[h, pl.ds(0, n_ka - 1)]
        return pltpu.make_async_remote_copy(
            src_ref=span, dst_ref=span, send_sem=send_sem, recv_sem=recv_sem,
            device_id={"vib": other}, device_id_type=MESH,
        )

    def add_sums(h):
        all_out(zrecv, h, out_send, out_recv.at[h]).wait_recv()
        all_out(srecv, h, scale_send, scale_recv.at[h]).wait_recv()
        total = out_ref[:, half_lanes(h)]
        for d in range(1, n_ka):
            sender = lax.rem(a + d, n_ka)
            total = total + zrecv[h, sender].astype(F32) * srecv[h, sender]
        out_ref[:, half_lanes(h)] = total

    own_half(0, 0)
    if n_half > 1:
        own_half(0, 1)
    own_half(1, 0)
    if n_half > 1:
        own_half(1, 1)
    for j in chunks(0):
        if j == len(cuts[0]) - 2:
            turn_initial()

            @pl.when(b == 1)
            def _():
                for h in range(1, n_half):
                    start_edges(h)
        relay(0, j)
        if j == 0 and rounds > 0:
            for side in range(2):
                token(side, 1)
    for side in range(2):
        @pl.when(takes[side])
        def _():
            count_copy(side).wait_recv()
    for h in range(n_half):
        if h == 0:
            take(h, b, 0, rows)
            for j in chunks(h):
                forward(h, j).wait_recv()
            take(h, other, 0, rows, last_take=True)
            for r in range(1, rounds + 1):
                for side in range(2):
                    if r > 1:
                        token(side, r)
                for side in range(2):
                    await_token(side, r)
        else:
            for j in chunks(h):
                relay(h, j)
                take(h, b, *chunk(h, j))
                if j > 1:
                    take_other(h, j - 2)
            for j in list(chunks(h))[-2:]:
                take_other(h, j)
        send_away(h)
        stay(h)
        finish(h)
    for h in range(n_half):
        add_sums(h)

    def drain():
        for side in range(2):
            @pl.when(sends[side])
            def _():
                count_copy(side).wait_send()
                pltpu.make_async_remote_copy(
                    src_ref=final_hbm.at[0], dst_ref=final_hbm.at[0],
                    send_sem=z_send.at[side], recv_sem=z_recv.at[side, 0, 0],
                    device_id={"vib": other}, device_id_type=MESH,
                ).wait_send()
        for h in range(n_half):
            own_copy(h).wait_send()
            all_out(zsend, h, out_send, out_recv.at[h]).wait_send()
            all_out(ssend, h, scale_send, scale_recv.at[h]).wait_send()
        for buffer, sem in ((edge.at[:, rows_of(b)], fwd_send), (away, part_send), (away_scale, part_scale_send)):
            pltpu.make_async_remote_copy(
                src_ref=buffer, dst_ref=buffer, send_sem=sem, recv_sem=sem,
                device_id={"vib": other}, device_id_type=MESH,
            ).wait_send()

    drain()


def on_device(n_ka, moments, initial_vectors, final_vectors, basis_counts):
    kblocks, rows, states = initial_vectors.shape
    width = final_vectors.shape[2]
    whole = moments.shape[2]
    share = states // (2 * n_ka)
    n_half = max(1, width // 128)
    half = width // n_half
    cuts = [[0, rows // 2, rows]] * n_half
    most = max(len(c) for c in cuts) - 1
    groups = 2
    dma = pltpu.SemaphoreType.DMA
    vmem = pltpu.VMEM
    amplitude = pl.pallas_call(
        functools.partial(kernel, n_ka, n_half, cuts, groups),
        out_shape=vmem((share, width), F32),
        in_specs=[pl.BlockSpec(memory_space=pl.ANY)] * 4,
        out_specs=pl.BlockSpec(memory_space=pltpu.VMEM),
        scratch_shapes=[
            pltpu.SMEM((kblocks,), jnp.int32),
            vmem(moments.shape, BF16),
            vmem(initial_vectors.shape, BF16),
            vmem((2, n_ka * share, kblocks * rows), BF16),
            vmem((n_half, kblocks, whole, half), BF16),
            vmem((n_half, whole, 2 * half), BF16),
            vmem((n_half, rows, kblocks * half), F32),
            vmem((n_half, kblocks * rows, 2 * half), BF16),
            vmem((n_half, n_ka * share, half), jnp.int16),
            vmem((n_half, groups, 1, half), F32),
            vmem((n_ka * share, half), F32),
            vmem((n_half, n_ka * share, half), jnp.int16),
            vmem((n_half, groups, 1, half), F32),
            vmem((n_half, n_ka, share, half), jnp.int16),
            vmem((n_half, n_ka, share, half), jnp.int16),
            vmem((n_half, n_ka, 1, half), F32),
            vmem((n_half, n_ka, 1, half), F32),
            vmem((2, 8, half), jnp.int32),
            vmem((2, 8, half), jnp.int32),
            dma(()),
            dma((2,)),
            dma(()),
            dma((n_half,)),
            dma((n_half,)),
            dma((n_half,)),
            dma((2,)),
            dma((2, n_half, most)),
            dma((2,)),
            dma((2,)),
            dma(()),
            dma((n_half, most)),
            dma(()),
            dma((n_half,)),
            dma(()),
            dma((n_half,)),
            dma(()),
            dma((n_half,)),
            dma(()),
            dma((n_half,)),
            pltpu.SemaphoreType.REGULAR((max(1, n_ka - 3),)),
            pltpu.SemaphoreType.REGULAR((max(1, n_ka - 3),)),
        ],
        compiler_params=pltpu.CompilerParams(
            collective_id=0, has_side_effects=True, vmem_limit_bytes=60 * 2**20
        ),
    )(basis_counts, moments, initial_vectors, final_vectors)
    return amplitude * amplitude


def solution(mesh):
    in_specs = (
        P(None, "vib", None),
        P("ka", "vib", "grp"),
        P("ka", "vib", ("grp", "fin")),
        P(("grp", "ka")),
    )
    out_specs = P(("grp", "ka", "vib"), "fin")
    return jax.shard_map(
        functools.partial(on_device, mesh.shape["ka"]),
        mesh=mesh, in_specs=in_specs, out_specs=out_specs, check_vma=False,
    )
```

```python
import functools
import math

import jax
import jax.numpy as jnp
from jax import lax
from jax.experimental import pallas as pl
from jax.experimental.pallas import tpu as pltpu
from jax.sharding import PartitionSpec as P

JQ = 30
MESH = pl.DeviceIdType.MESH
F32 = jnp.float32
BF16 = jnp.bfloat16
LEVELS = 32767.0
TINY = 1e-30


def coefficient_rows(index, width):
    value = jnp.full((1, width), index, jnp.int32).astype(F32)
    jsquare = float(JQ * (JQ + 1))
    norm_j = jnp.sqrt(jnp.full((1, width), jsquare, F32))
    same = value / norm_j
    upper = 0.5 * jnp.sqrt(jsquare - value * (value + 1.0)) / norm_j
    lower = -0.5 * jnp.sqrt(jsquare - value * (value - 1.0)) / norm_j
    return same, upper, lower


def kernel(
    n_ka, n_half, cuts, groups, counts_hbm, moments_hbm, initial_hbm, final_hbm, out_ref,
    counts, mom, ini, turned, own, edge, comb, split, away, mine, part, zsend, zrecv, ssend, srecv, csend, crecv,
    counts_sem, mom_sem, ini_sem, own_sem, own_send, own_recv, z_send, z_recv, count_send, count_recv,
    fwd_send, fwd_recv, part_send, part_recv, out_send, out_recv, scale_send, scale_recv,
    token_up, token_down,
):
    kblocks, rows, states = ini.shape
    width = final_hbm.shape[2]
    share = out_ref.shape[0]
    whole = mom.shape[2]
    half = width // n_half
    last = kblocks - 1
    tile = min(256, rows)
    a = lax.axis_index("ka")
    b = lax.axis_index("vib")
    other = 1 - b
    first = a * kblocks - kblocks * n_ka // 2
    cores = (b, other)
    has_up = a < n_ka - 1
    has_down = a > 0
    sends = (has_up, has_down)
    takes = (has_down, has_up)
    toward_side = (a + 1, a - 1)

    barrier = pltpu.get_barrier_semaphore()
    pl.semaphore_signal(barrier, inc=1, device_id={"vib": other}, device_id_type=MESH)
    for side in range(2):
        @pl.when(sends[side])
        def _():
            pl.semaphore_signal(
                barrier, inc=1, device_id={"ka": toward_side[side]}, device_id_type=MESH
            )

    def rows_of(core):
        return pl.ds(pl.multiple_of(core * rows, rows), rows)

    def chunk(h, j):
        bounds = cuts[h]
        return bounds[j], bounds[j + 1] - bounds[j]

    def chunks(h):
        return range(len(cuts[h]) - 1)

    def at(core, h, j):
        low, count = chunk(h, j)
        return pl.ds(pl.multiple_of(core * rows + low, math.gcd(rows, low)), count)

    def half_lanes(i):
        return pl.ds(i * half, half)

    def get_own(h):
        return pltpu.make_async_copy(
            final_hbm.at[:, :, half_lanes(h)], own.at[h, :, rows_of(b)], own_sem.at[h]
        )

    def get_moments(i):
        span = rows_of(cores[i])
        return pltpu.make_async_copy(moments_hbm.at[:, :, span], mom.at[:, :, span], mom_sem.at[i])

    get_counts = pltpu.make_async_copy(counts_hbm, counts, counts_sem)
    get_initial = pltpu.make_async_copy(initial_hbm, ini, ini_sem)

    def own_copy(h):
        return pltpu.make_async_remote_copy(
            src_ref=final_hbm.at[:, :, half_lanes(h)],
            dst_ref=own.at[h, :, rows_of(b)],
            send_sem=own_send.at[h],
            recv_sem=own_recv.at[h],
            device_id={"vib": other},
            device_id_type=MESH,
        )

    def z_copy(side, h, j):
        return pltpu.make_async_remote_copy(
            src_ref=final_hbm.at[last * (1 - side), pl.ds(*chunk(h, j)), half_lanes(h)],
            dst_ref=edge.at[h, at(b, h, j), half_lanes(side)],
            send_sem=z_send.at[side],
            recv_sem=z_recv.at[side, h, j],
            device_id={"ka": toward_side[side]},
            device_id_type=MESH,
        )

    def count_copy(side):
        return pltpu.make_async_remote_copy(
            src_ref=csend.at[side],
            dst_ref=crecv.at[side],
            send_sem=count_send.at[side],
            recv_sem=count_recv.at[side],
            device_id={"ka": toward_side[side]},
            device_id_type=MESH,
        )

    def forward(h, j):
        return pltpu.make_async_remote_copy(
            src_ref=edge.at[h, at(b, h, j)],
            dst_ref=edge.at[h, at(b, h, j)],
            send_sem=fwd_send,
            recv_sem=fwd_recv.at[h, j],
            device_id={"vib": other},
            device_id_type=MESH,
        )

    def start_edges(h):
        for j in chunks(h):
            for side in range(2):
                @pl.when(sends[side])
                def _():
                    z_copy(side, h, j).start()

    def start_loads():
        get_counts.start()
        for h in range(n_half):
            get_own(h).start()
        for i in range(2):
            get_moments(i).start()

    def greet():
        for side in range(2):
            @pl.when(jnp.logical_not(takes[side]))
            def _():
                crecv[side] = jnp.zeros(crecv.shape[1:], jnp.int32)
                for h in range(n_half):
                    edge[h, rows_of(b), side * half : (side + 1) * half] = jnp.zeros((rows, half), BF16)
        get_counts.wait()
        for side in range(2):
            csend[side] = jnp.full(csend.shape[1:], counts[last * (1 - side)], jnp.int32)
        pl.semaphore_wait(barrier, 1 + has_up.astype(jnp.int32) + has_down.astype(jnp.int32))
        for side in range(2):
            @pl.when(sends[side])
            def _():
                count_copy(side).start()
        start_edges(0)
        for h in range(n_half):
            own_copy(h).start()

        @pl.when(b == 0)
        def _():
            for h in range(1, n_half):
                start_edges(h)

    start_loads()
    greet()

    same0, upper0, _ = coefficient_rows(first, half)
    same1, _, lower1 = coefficient_rows(first + 1, half)
    _, upper_below, _ = coefficient_rows(first - 1, half)
    _, _, lower_above = coefficient_rows(first + 2, half)
    same_row = jnp.concatenate([same0, same1], axis=1)
    cross_row = jnp.concatenate([lower1, upper0], axis=1)
    edge_row = jnp.concatenate([upper_below, lower_above], axis=1)

    rounds = max(0, n_ka - 3)

    def token(side, r):
        sem = (token_up, token_down)[side]
        known = a - 1 - r >= 0 if side == 0 else a + 1 + r <= n_ka - 1

        @pl.when(jnp.logical_and(known, sends[side]))
        def _():
            pl.semaphore_signal(
                sem.at[r - 1], inc=1, device_id={"ka": toward_side[side]}, device_id_type=MESH
            )

    def await_token(side, r):
        sem = (token_up, token_down)[side]

        @pl.when(a - 2 - r >= 0 if side == 0 else a + 2 + r <= n_ka - 1)
        def _():
            pl.semaphore_wait(sem.at[r - 1], 1)

    def relay(h, j):
        for side in range(2):
            @pl.when(takes[side])
            def _():
                z_copy(side, h, j).wait_recv()
        forward(h, j).start()

    def own_half(i, h):
        row_index = lax.broadcasted_iota(jnp.int32, (rows, half), 0) + cores[i] * rows
        if i == 0:
            get_own(h).wait()
        else:
            own_copy(h).wait_recv()
        masked = []
        for k in range(kblocks):
            piece = own[h, k, rows_of(cores[i]), :].astype(F32)
            masked.append(jnp.where(row_index < counts[k], piece, 0.0).astype(BF16))
        piece = jnp.concatenate(masked, axis=1)
        if h == 0:
            get_moments(i).wait()
            if i == 0:
                get_initial.start()
        for t in range(rows // tile):
            span = pl.ds(t * tile, tile)
            along_z = jnp.dot(mom[0, span, rows_of(cores[i])], piece, preferred_element_type=F32)
            along_x = jnp.dot(mom[1, span, rows_of(cores[i])], piece, preferred_element_type=F32)
            crossed = jnp.concatenate([along_x[:, half:], along_x[:, :half]], axis=1)
            value = same_row * along_z + cross_row * crossed
            comb[h, span, :] = value if i == 0 else comb[h, span, :] + value

    def turn_initial():
        get_initial.wait()
        for k in range(kblocks):
            for v in range(rows // tile):
                block = ini[k, v * tile : (v + 1) * tile, :].T
                low = k * rows + v * tile
                for target in range(n_ka):
                    for core in range(2):
                        start = (target * 2 + core) * share
                        turned[core, target * share : (target + 1) * share, low : low + tile] = block[
                            start : start + share
                        ]

    row_index = lax.broadcasted_iota(jnp.int32, (tile, half), 0) + b * rows

    def take(h, core, low, size, last_take=False):
        start = core * rows + low
        edge_index = lax.broadcasted_iota(jnp.int32, (size, 2 * half), 0)
        edge_counts = jnp.concatenate([crecv[0, 0:1, :], crecv[1, 0:1, :]], axis=1)
        span_w = pl.ds(pl.multiple_of(start, math.gcd(rows, low)), size)
        piece = edge[h, span_w, :].astype(F32)
        piece = jnp.where(edge_index + start < edge_counts, piece, 0.0).astype(BF16)
        for t in range(rows // tile):
            span = pl.ds(t * tile, tile)
            value = comb[h, span, :] + edge_row * jnp.dot(
                mom[1, span, span_w], piece, preferred_element_type=F32
            )
            if not last_take:
                comb[h, span, :] = value
                continue
            for k in range(kblocks):
                live = jnp.where(
                    row_index + t * tile < counts[k], value[:, k * half : (k + 1) * half], 0.0
                )
                high = live.astype(BF16)
                start_v = k * rows + t * tile
                split[h, start_v : start_v + tile, 0:half] = high
                split[h, start_v : start_v + tile, half:] = (live - high.astype(F32)).astype(BF16)

    def take_other(h, j):
        forward(h, j).wait_recv()
        take(h, other, *chunk(h, j), last_take=j == len(cuts[h]) - 2)

    targets = n_ka // groups
    size = targets * share

    def part_copy(h):
        return pltpu.make_async_remote_copy(
            src_ref=away.at[h],
            dst_ref=part.at[h],
            send_sem=part_send,
            recv_sem=part_recv.at[h],
            device_id={"vib": other},
            device_id_type=MESH,
        )

    def out_copies(h, sender, target):
        values = pltpu.make_async_remote_copy(
            src_ref=zsend.at[h, target],
            dst_ref=zrecv.at[h, sender],
            send_sem=out_send,
            recv_sem=out_recv.at[h],
            device_id={"ka": target},
            device_id_type=MESH,
        )
        scales = pltpu.make_async_remote_copy(
            src_ref=ssend.at[h, target],
            dst_ref=srecv.at[h, sender],
            send_sem=scale_send,
            recv_sem=scale_recv.at[h],
            device_id={"ka": target},
            device_id_type=MESH,
        )
        return values, scales

    def amplitude(h, core):
        parts = []
        for g in range(groups):
            both = jnp.dot(
                turned[core, g * size : (g + 1) * size, :], split[h], preferred_element_type=F32
            )
            parts.append(both[:, :half] + both[:, half:])
        return parts

    def send_away(h):
        for g, value in enumerate(amplitude(h, other)):
            away[h, g * size : (g + 1) * size, :] = value
        part_copy(h).start()

    def stay(h):
        for g, value in enumerate(amplitude(h, b)):
            mine[g * size : (g + 1) * size, :] = value

    upper_half = (2 * a) // n_ka

    def finish(h):
        part_copy(h).wait_recv()
        for i in range(n_ka):
            target = upper_half * i + (1 - upper_half) * (n_ka - 1 - i)
            span = pl.ds(pl.multiple_of(target * share, share), share)
            value = mine[span, :] + part[h, span, :]

            @pl.when(target == a)
            def _():
                out_ref[:, half_lanes(h)] = value

            @pl.when(target != a)
            def _():
                peak = jnp.maximum(jnp.max(jnp.abs(value), axis=0, keepdims=True), TINY)
                zsend[h, target] = jnp.round(value * (LEVELS / peak)).astype(jnp.int16)
                ssend[h, target] = peak / LEVELS
                for copy in out_copies(h, a, target):
                    copy.start()

    def all_out(ref, h, send_sem, recv_sem):
        span = ref.at[h, pl.ds(0, n_ka - 1)]
        return pltpu.make_async_remote_copy(
            src_ref=span, dst_ref=span, send_sem=send_sem, recv_sem=recv_sem,
            device_id={"vib": other}, device_id_type=MESH,
        )

    def add_sums(h):
        all_out(zrecv, h, out_send, out_recv.at[h]).wait_recv()
        all_out(srecv, h, scale_send, scale_recv.at[h]).wait_recv()
        total = out_ref[:, half_lanes(h)]
        for d in range(1, n_ka):
            sender = lax.rem(a + d, n_ka)
            total = total + zrecv[h, sender].astype(F32) * srecv[h, sender]
        out_ref[:, half_lanes(h)] = total

    own_half(0, 0)
    if n_half > 1:
        own_half(0, 1)
    own_half(1, 0)
    if n_half > 1:
        own_half(1, 1)
    for j in chunks(0):
        if j == len(cuts[0]) - 2:
            turn_initial()

            @pl.when(b == 1)
            def _():
                for h in range(1, n_half):
                    start_edges(h)
        relay(0, j)
        if j == 0 and rounds > 0:
            for side in range(2):
                token(side, 1)
    for side in range(2):
        @pl.when(takes[side])
        def _():
            count_copy(side).wait_recv()
    for h in range(n_half):
        if h == 0:
            take(h, b, 0, rows)
            for j in chunks(h):
                forward(h, j).wait_recv()
            take(h, other, 0, rows, last_take=True)
            for r in range(1, rounds + 1):
                for side in range(2):
                    if r > 1:
                        token(side, r)
                for side in range(2):
                    await_token(side, r)
        else:
            for j in chunks(h):
                relay(h, j)
                take(h, b, *chunk(h, j))
                if j > 1:
                    take_other(h, j - 2)
            for j in list(chunks(h))[-2:]:
                take_other(h, j)
        send_away(h)
        stay(h)
        finish(h)
    for h in range(n_half):
        add_sums(h)

    def drain():
        for side in range(2):
            @pl.when(sends[side])
            def _():
                count_copy(side).wait_send()
                pltpu.make_async_remote_copy(
                    src_ref=final_hbm.at[0], dst_ref=final_hbm.at[0],
                    send_sem=z_send.at[side], recv_sem=z_recv.at[side, 0, 0],
                    device_id={"vib": other}, device_id_type=MESH,
                ).wait_send()
        for h in range(n_half):
            own_copy(h).wait_send()
            all_out(zsend, h, out_send, out_recv.at[h]).wait_send()
            all_out(ssend, h, scale_send, scale_recv.at[h]).wait_send()
        for buffer, sem in ((edge.at[:, rows_of(b)], fwd_send), (away, part_send)):
            pltpu.make_async_remote_copy(
                src_ref=buffer, dst_ref=buffer, send_sem=sem, recv_sem=sem,
                device_id={"vib": other}, device_id_type=MESH,
            ).wait_send()

    drain()


def on_device(n_ka, moments, initial_vectors, final_vectors, basis_counts):
    kblocks, rows, states = initial_vectors.shape
    width = final_vectors.shape[2]
    whole = moments.shape[2]
    share = states // (2 * n_ka)
    n_half = max(1, width // 128)
    half = width // n_half
    cuts = [[0, rows // 2, rows]] * n_half
    most = max(len(c) for c in cuts) - 1
    groups = 2
    dma = pltpu.SemaphoreType.DMA
    vmem = pltpu.VMEM
    amplitude = pl.pallas_call(
        functools.partial(kernel, n_ka, n_half, cuts, groups),
        out_shape=vmem((share, width), F32),
        in_specs=[pl.BlockSpec(memory_space=pl.ANY)] * 4,
        out_specs=pl.BlockSpec(memory_space=pltpu.VMEM),
        scratch_shapes=[
            pltpu.SMEM((kblocks,), jnp.int32),
            vmem(moments.shape, BF16),
            vmem(initial_vectors.shape, BF16),
            vmem((2, n_ka * share, kblocks * rows), BF16),
            vmem((n_half, kblocks, whole, half), BF16),
            vmem((n_half, whole, 2 * half), BF16),
            vmem((n_half, rows, kblocks * half), F32),
            vmem((n_half, kblocks * rows, 2 * half), BF16),
            vmem((n_half, n_ka * share, half), F32),
            vmem((n_ka * share, half), F32),
            vmem((n_half, n_ka * share, half), F32),
            vmem((n_half, n_ka, share, half), jnp.int16),
            vmem((n_half, n_ka, share, half), jnp.int16),
            vmem((n_half, n_ka, 1, half), F32),
            vmem((n_half, n_ka, 1, half), F32),
            vmem((2, 8, half), jnp.int32),
            vmem((2, 8, half), jnp.int32),
            dma(()),
            dma((2,)),
            dma(()),
            dma((n_half,)),
            dma((n_half,)),
            dma((n_half,)),
            dma((2,)),
            dma((2, n_half, most)),
            dma((2,)),
            dma((2,)),
            dma(()),
            dma((n_half, most)),
            dma(()),
            dma((n_half,)),
            dma(()),
            dma((n_half,)),
            dma(()),
            dma((n_half,)),
            pltpu.SemaphoreType.REGULAR((max(1, n_ka - 3),)),
            pltpu.SemaphoreType.REGULAR((max(1, n_ka - 3),)),
        ],
        compiler_params=pltpu.CompilerParams(
            collective_id=0, has_side_effects=True, vmem_limit_bytes=60 * 2**20
        ),
    )(basis_counts, moments, initial_vectors, final_vectors)
    return amplitude * amplitude


def solution(mesh):
    in_specs = (
        P(None, "vib", None),
        P("ka", "vib", "grp"),
        P("ka", "vib", ("grp", "fin")),
        P(("grp", "ka")),
    )
    out_specs = P(("grp", "ka", "vib"), "fin")
    return jax.shard_map(
        functools.partial(on_device, mesh.shape["ka"]),
        mesh=mesh, in_specs=in_specs, out_specs=out_specs, check_vma=False,
    )
```
